32 devices in a mesh: groups: 2 (over y), seq: 4 (over z), head: 2 (over x), sub: 2 (over core).
Axes of the slice: x: 2, y: 2, z: 4, core: 2. Of those that a mesh axis runs over, the one named last changes fastest.
Arguments:
- hidden_states: bfloat16 [8192, 8192], P(('groups', 'seq', 'sub'), 'head'), parts along dimension 0, may hold values from -42 to 42
- key_projection_weight: bfloat16 [8192, 1024], P(('seq', 'sub'), 'head'), may hold values from -0.0625 to 0.0625
- value_projection_weight: bfloat16 [8192, 1024], P(('seq', 'sub'), 'head'), may hold values from -0.0625 to 0.0625
- head_basis_matrix: float32 [8, 128, 64], P('head'), may hold values from -0.5 to 0.5
- slot_token: int32 [8192], P(('groups', 'seq', 'sub')), parts along dimension 0, may hold values from 0 to 4095, as said below
Outputs:
- compressed_keys: bfloat16 [8192, 512], P(('groups', 'seq', 'sub'), 'head'), parts along dimension 0
- value_cache: bfloat16 [8192, 1024], P(('groups', 'seq', 'sub'), 'head'), parts along dimension 0
The draws below stay inside these ranges and needn't reach their ends.
There are 2 independent parts, one for each index of `groups`. The reference program is written for one: setup_inputs(seed, part) draws one part's arguments, and reference() takes and returns one part's arrays. A program takes and returns all parts, laid end to end along the dimension named above; an argument that names none is the same for every part. Nothing has to cross between parts.
Inputs may be any that keep to these rules, and one draw needn't show every extreme that they name: `slot_token`: A permutation of the 4096 token positions. Each aligned block of 512 rows holds exactly 64 positions of each aligned block of 512 positions.
All inputs are finite; a program needn't handle non-finite values.
Results may differ from the reference program's by a relative error of at most 0.0055.
Values may be sent and summed in bfloat16 or wider, within the bound.
No kernel may reach another device: no remote copies, remote signals or barrier semaphores. Data moves between devices by JAX's collectives and lax.ppermute only.
A program may use at most 64 MiB of HBM per device.

```python
import jax
import jax.numpy as jnp
from jax import lax

MODEL_WIDTH = 8192
KEY_VALUE_HEADS = 8
HEAD_SIZE = 128
BASIS_RANK = 64
TOK_DEV = 512
WINDOW_TOKENS = 4096


def draw_hidden_states(key, part):
    base_key, row_key, col_key = jax.random.split(key, 3)
    quarter_rows = WINDOW_TOKENS // 4
    position = jnp.arange(WINDOW_TOKENS, dtype=jnp.float32) / WINDOW_TOKENS
    row_scale = jnp.exp(jnp.log(3.0) * (position - 0.5) + jax.random.uniform(row_key, (WINDOW_TOKENS,), jnp.float32, -0.6, 0.6))
    col_scale = jnp.exp(jax.random.uniform(col_key, (4, MODEL_WIDTH), jnp.float32, -1.15, 1.15))
    base = jax.random.truncated_normal(base_key, -4.0, 4.0, (4, quarter_rows, MODEL_WIDTH), jnp.float32)
    scaled = (base * col_scale[:, None, :]).reshape(WINDOW_TOKENS, MODEL_WIDTH) * row_scale[:, None]
    return scaled.astype(jnp.bfloat16)


def shuffle_one(subkey):
    return jax.random.permutation(subkey, TOK_DEV)


def draw_slot_token(key, part):
    blocks = WINDOW_TOKENS // TOK_DEV
    share = TOK_DEV // blocks
    first_key, second_key = jax.random.split(key)
    local_order = jax.vmap(shuffle_one)(jax.random.split(first_key, blocks)).astype(jnp.int32)
    positions = local_order + jnp.arange(blocks, dtype=jnp.int32)[:, None] * TOK_DEV
    grouped = jnp.transpose(positions.reshape(blocks, blocks, share), (1, 0, 2)).reshape(blocks, TOK_DEV)
    shuffle = jax.vmap(shuffle_one)(jax.random.split(second_key, blocks)).astype(jnp.int32)
    return jnp.take_along_axis(grouped, shuffle, axis=1).reshape(WINDOW_TOKENS).astype(jnp.int32)


def block_levels(key, shape, cuts, low, largest):
    def one(axis_at, parts):
        steps = jax.random.uniform(jax.random.fold_in(jax.random.fold_in(key, 6), axis_at), (parts,), jnp.float32, low / len(cuts), largest / len(cuts))
        return jnp.repeat(jnp.exp(steps), shape[axis_at] // parts).reshape((-1,) + (1,) * (len(shape) - axis_at - 1))

    level = one(*cuts[0])
    for cut in cuts[1:]:
        level = level * one(*cut)
    return level


def noise(key, dims, width, most, cuts=(), kind=jnp.bfloat16):
    result = jax.random.normal(key, dims, jnp.float32) * width
    if len(cuts) > 0:
        result = block_levels(key, dims, cuts, -0.22, 0.18) * result
    return jnp.clip(result, min=-most, max=most).astype(kind)


def setup_inputs(seed: int = 0, part: int = 0) -> dict:
    key_list = jax.random.split(jax.random.key(seed), 6)
    part_splits = jax.random.split(jax.random.fold_in(key_list[5], part), 6)
    return {
        "hidden_states": draw_hidden_states(jax.random.fold_in(jax.random.fold_in(key_list[5], part), 71), part),
        "key_projection_weight": noise(key_list[1], (MODEL_WIDTH, KEY_VALUE_HEADS * HEAD_SIZE), MODEL_WIDTH ** -0.5, 0.0625, ((0, 8), (1, 2))),
        "value_projection_weight": noise(key_list[2], (MODEL_WIDTH, KEY_VALUE_HEADS * HEAD_SIZE), MODEL_WIDTH ** -0.5, 0.0625, ((0, 8), (1, 2))),
        "head_basis_matrix": noise(key_list[3], (KEY_VALUE_HEADS, HEAD_SIZE, BASIS_RANK), HEAD_SIZE ** -0.5, 0.5, ((0, 2),), jnp.float32),
        "slot_token": draw_slot_token(jax.random.fold_in(jax.random.fold_in(key_list[5], part), 71), part),
    }


ridge_share = 0.05

def reference(hidden_states, key_projection_weight, value_projection_weight, head_basis_matrix, slot_token):
    decode_key_cache = jnp.dot(hidden_states.astype(jnp.float32), key_projection_weight.astype(jnp.float32), preferred_element_type=jnp.float32).astype(jnp.bfloat16)
    values = jnp.dot(hidden_states.astype(jnp.float32), value_projection_weight.astype(jnp.float32), preferred_element_type=jnp.float32).astype(jnp.bfloat16)
    per_head_keys = decode_key_cache.astype(jnp.float32).reshape(WINDOW_TOKENS, KEY_VALUE_HEADS, HEAD_SIZE)
    moments = jnp.einsum('thi,thj->hij', per_head_keys, per_head_keys, precision=lax.Precision.HIGHEST) / WINDOW_TOKENS
    trace_vals = jnp.trace(moments, axis1=1, axis2=2)
    identity = jnp.eye(HEAD_SIZE, dtype=jnp.float32)
    regular = moments + (ridge_share * trace_vals / HEAD_SIZE)[:, None, None] * identity
    factor = jnp.linalg.cholesky(regular)
    by_head = jnp.transpose(per_head_keys, (1, 0, 2))
    whitened = lax.linalg.triangular_solve(factor, by_head, left_side=False, lower=True, transpose_a=True)
    basis_coefficients = jnp.einsum('htd,hdr->htr', whitened, head_basis_matrix, precision=lax.Precision.HIGHEST)
    basis_coefficients = jnp.transpose(basis_coefficients, (1, 0, 2)).reshape(WINDOW_TOKENS, KEY_VALUE_HEADS * BASIS_RANK).astype(jnp.bfloat16)
    return (basis_coefficients[slot_token], values[slot_token])
```

```python
import functools

import jax
import jax.numpy as jnp
from jax import lax
from jax.experimental import pallas as pl
from jax.experimental.pallas import tpu as pltpu
from jax.sharding import PartitionSpec as P

ridge_share = 0.05
SWAP = [(0, 1), (1, 0)]


def rotation(count, shift):
    return [(i, (i + shift) % count) for i in range(count)]


def solve_kernel(scale, parts, *refs):
    m_refs, basis_ref, out_ref = refs[:parts], refs[parts], refs[parts + 1]
    heads, dim, _ = basis_ref.shape
    total = m_refs[0][...]
    for ref in m_refs[1:]:
        total = total + ref[...]
    total = total * scale
    row = lax.broadcasted_iota(jnp.int32, (1, dim, dim), 1)
    col = lax.broadcasted_iota(jnp.int32, (1, dim, dim), 2)
    diag = row == col
    trace = jnp.sum(jnp.where(diag, total, 0.0), axis=(1, 2), keepdims=True)
    work = total + jnp.where(diag, ridge_share * trace / dim, 0.0)
    tiles = [work[:, r : r + 8, :] for r in range(0, dim, 8)]
    lane = lax.broadcasted_iota(jnp.int32, (1, 1, dim), 2)
    sub = lax.broadcasted_iota(jnp.int32, (1, 8, 1), 1)
    for j in range(dim):
        t0, j0 = j // 8, j % 8
        pivot_row = tiles[t0][:, j0 : j0 + 1, :]
        inv = 1.0 / pivot_row[:, :, j : j + 1]
        scaled = jnp.where(lane == j, inv, pivot_row * inv)
        at = lane == j
        for t in range(t0, dim // 8):
            if t == t0 and j0 == 7:
                continue
            f = tiles[t][:, :, j : j + 1]
            if t == t0:
                f = jnp.where(sub > j0, f, 0.0)
                base = jnp.where(at & (sub > j0), 0.0, tiles[t])
            else:
                base = jnp.where(at, 0.0, tiles[t])
            tiles[t] = base - f * scaled
    work = jnp.concatenate(tiles, axis=1)
    pivots = jnp.sum(jnp.where(diag, work, 0.0), axis=2, keepdims=True)
    inverse = jnp.where(row > col, work, jnp.where(diag, 1.0, 0.0))
    scaled_basis = basis_ref[...] * lax.rsqrt(pivots)
    for h in range(heads):
        out_ref[h] = lax.dot_general(
            inverse[h].T,
            scaled_basis[h],
            (((1,), (0,)), ((), ())),
            precision=lax.Precision.HIGHEST,
            preferred_element_type=jnp.float32,
        )


def solve(parts, basis, token_total):
    heads, dim, rank = basis.shape
    vmem = pl.BlockSpec(memory_space=pltpu.VMEM)
    return pl.pallas_call(
        functools.partial(solve_kernel, 1.0 / token_total, len(parts)),
        out_shape=jax.ShapeDtypeStruct((heads, dim, rank), jnp.float32),
        in_specs=[vmem] * (len(parts) + 1),
        out_specs=vmem,
        cost_estimate=pl.CostEstimate(flops=heads * dim**3, bytes_accessed=4 * heads * dim * dim, transcendentals=0),
    )(*parts, basis)


def per_device(hidden_states, key_w, value_w, basis, slot):
    tokens = hidden_states.shape[0]
    seq, head, cores = lax.axis_size("seq"), lax.axis_size("head"), lax.axis_size("sub")
    h_at, c_at = lax.axis_index("head"), lax.axis_index("sub")
    peers = seq * cores
    share = tokens // peers
    heads, dim, rank = basis.shape
    width = heads * dim

    block = slot // tokens
    place = lax.iota(jnp.int32, tokens)
    before = (block[None, :] == block[:, None]) & (place[None, :] < place[:, None])
    position = block * share + jnp.sum(before.astype(jnp.int32), axis=1)
    hits = position[:, None] == place[None, :]
    wanted = jnp.sum(jnp.where(hits, (slot - block * tokens)[:, None], 0), axis=0)
    asked = lax.all_to_all(wanted, ("seq", "sub"), split_axis=0, concat_axis=0, tiled=True)
    pick = (asked[:, None] == place[None, :]).astype(jnp.bfloat16)
    unpick = hits.astype(jnp.bfloat16)

    feats = hidden_states.shape[1]
    weights = lax.all_gather(
        jnp.concatenate([key_w, value_w], axis=1), ("seq", "sub"), axis=0, tiled=True
    )
    sums = None
    for d in range(head):
        x = hidden_states if d == 0 else lax.ppermute(hidden_states, "head", rotation(head, -d))
        w = lax.dynamic_slice_in_dim(weights, lax.rem(h_at + d, head) * feats, feats, axis=0)
        term = jnp.dot(x, w, preferred_element_type=jnp.float32)
        sums = term if sums is None else sums + term
    both = sums.astype(jnp.bfloat16)
    keys = both[:, :width].reshape(tokens, heads, dim)

    mine = heads // cores
    local = jnp.einsum("thi,thj->hij", keys, keys, preferred_element_type=jnp.float32)
    local = local.reshape(cores, mine, dim, dim)
    chip = lax.dynamic_index_in_dim(local, c_at, 0, keepdims=False) + lax.ppermute(
        lax.dynamic_index_in_dim(local, 1 - c_at, 0, keepdims=False), "sub", SWAP
    )
    parts = [chip] + [lax.ppermute(chip, "seq", rotation(seq, d)) for d in range(1, seq)]
    basis_here = lax.dynamic_slice_in_dim(basis, c_at * mine, mine, axis=0)
    solved = solve(parts, basis_here, tokens * peers)
    other = lax.ppermute(solved, "sub", SWAP)
    maps = jnp.where(
        c_at == 0, jnp.concatenate([solved, other]), jnp.concatenate([other, solved])
    )

    sent = jnp.dot(pick, both, preferred_element_type=jnp.float32).astype(jnp.bfloat16)
    got = lax.all_to_all(sent, ("seq", "sub"), split_axis=0, concat_axis=0, tiled=True)
    rows = jnp.dot(unpick, got, preferred_element_type=jnp.float32).astype(jnp.bfloat16)
    coeffs = jnp.einsum(
        "thd,hdr->thr",
        rows[:, :width].astype(jnp.float32).reshape(tokens, heads, dim),
        maps,
        precision=lax.Precision.HIGHEST,
    )
    return coeffs.reshape(tokens, heads * rank).astype(jnp.bfloat16), rows[:, width:]


def solution(mesh):
    return jax.shard_map(
        per_device,
        mesh=mesh,
        in_specs=(
            P(("groups", "seq", "sub"), "head"),
            P(("seq", "sub"), "head"),
            P(("seq", "sub"), "head"),
            P("head", None, None),
            P(("groups", "seq", "sub")),
        ),
        out_specs=(P(("groups", "seq", "sub"), "head"), P(("groups", "seq", "sub"), "head")),
        check_vma=False,
    )
```

```python
import functools

import jax
import jax.numpy as jnp
from jax import lax
from jax.experimental import pallas as pl
from jax.experimental.pallas import tpu as pltpu
from jax.sharding import PartitionSpec as P

ridge_share = 0.05
SWAP = [(0, 1), (1, 0)]


def rotation(count, shift):
    return [(i, (i + shift) % count) for i in range(count)]


def xor(count, distance):
    return [(i, i ^ distance) for i in range(count)]


def pack(moments):
    first, second = moments[..., 0, :, :], moments[..., 1, :, :]
    dim = first.shape[-1]
    row = lax.broadcasted_iota(jnp.int32, (dim, dim), 0)
    col = lax.broadcasted_iota(jnp.int32, (dim, dim), 1)
    both = jnp.where(row >= col, first, second)
    diagonal = jnp.sum(jnp.where(row == col, second, 0.0), axis=-2, keepdims=True)
    return jnp.concatenate([both, jnp.broadcast_to(diagonal, (*both.shape[:-2], 8, dim))], axis=-2)


def unpack(packed):
    dim = packed.shape[1]
    row = lax.broadcasted_iota(jnp.int32, (dim, dim), 0)
    col = lax.broadcasted_iota(jnp.int32, (dim, dim), 1)
    both, diagonal = packed[:dim], packed[dim : dim + 1]
    turned = both.T
    first = jnp.where(row >= col, both, turned)
    second = jnp.where(row < col, both, jnp.where(row == col, diagonal, turned))
    return jnp.stack([first, second])


def solve_kernel(scale, parts, packed, *refs):
    m_refs, basis_ref, out_ref = refs[:parts], refs[parts], refs[parts + 1]
    heads, dim, _ = basis_ref.shape
    total = m_refs[0][...]
    for ref in m_refs[1:]:
        total = total + ref[...]
    total = total * scale
    if packed:
        total = unpack(total)
    row = lax.broadcasted_iota(jnp.int32, (1, dim, dim), 1)
    col = lax.broadcasted_iota(jnp.int32, (1, dim, dim), 2)
    diag = row == col
    trace = jnp.sum(jnp.where(diag, total, 0.0), axis=(1, 2), keepdims=True)
    work = total + jnp.where(diag, ridge_share * trace / dim, 0.0)
    tiles = [work[:, r : r + 8, :] for r in range(0, dim, 8)]
    lane = lax.broadcasted_iota(jnp.int32, (1, 1, dim), 2)
    sub = lax.broadcasted_iota(jnp.int32, (1, 8, 1), 1)
    for j in range(dim):
        t0, j0 = j // 8, j % 8
        pivot_row = tiles[t0][:, j0 : j0 + 1, :]
        inv = 1.0 / pivot_row[:, :, j : j + 1]
        scaled = jnp.where(lane == j, inv, pivot_row * inv)
        at = lane == j
        for t in range(t0, dim // 8):
            if t == t0 and j0 == 7:
                continue
            f = tiles[t][:, :, j : j + 1]
            if t == t0:
                f = jnp.where(sub > j0, f, 0.0)
                base = jnp.where(at & (sub > j0), 0.0, tiles[t])
            else:
                base = jnp.where(at, 0.0, tiles[t])
            tiles[t] = base - f * scaled
    work = jnp.concatenate(tiles, axis=1)
    pivots = jnp.sum(jnp.where(diag, work, 0.0), axis=2, keepdims=True)
    inverse = jnp.where(row > col, work, jnp.where(diag, 1.0, 0.0))
    scaled_basis = basis_ref[...] * lax.rsqrt(pivots)
    for h in range(heads):
        out_ref[h] = lax.dot_general(
            inverse[h].T,
            scaled_basis[h],
            (((1,), (0,)), ((), ())),
            precision=lax.Precision.HIGHEST,
            preferred_element_type=jnp.float32,
        )


def solve(parts, basis, token_total):
    heads, dim, rank = basis.shape
    vmem = pl.BlockSpec(memory_space=pltpu.VMEM)
    return pl.pallas_call(
        functools.partial(solve_kernel, 1.0 / token_total, len(parts), parts[0].ndim == 2),
        out_shape=jax.ShapeDtypeStruct((heads, dim, rank), jnp.float32),
        in_specs=[vmem] * (len(parts) + 1),
        out_specs=vmem,
        cost_estimate=pl.CostEstimate(flops=heads * dim**3, bytes_accessed=4 * heads * dim * dim, transcendentals=0),
    )(*parts, basis)


ALL_PIECES = [(d, k) for d in (1, 2, 3) for k in range(4)]
EARLY_PIECES = [(1, 0), (1, 1), (1, 2), (1, 3), (2, 0), (2, 2), (3, 0), (3, 2)]


def project_kernel(near, widths, last, *refs):
    refs = list(refs)
    x_own, xs = refs.pop(0), [refs.pop(0) for _ in widths]
    own, sib = refs.pop(0), refs.pop(0)
    pieces = {name: refs.pop(0) for name in (ALL_PIECES if last else EARLY_PIECES)}
    if last:
        acc_in, out_ref, xbuf, wbuf, xsem, wsem, acc, asem = refs
    else:
        acc, xbuf, wbuf, xsem, wsem = refs
    g, s, h, c = (lax.axis_index(a) for a in ("groups", "seq", "head", "sub"))
    block = own.shape[0]
    half = block // 2
    blocks = 2 * near
    far_early = sum(widths) - (widths[-1] if last else 0)

    def x_copy(src, at):
        lanes = pl.ds(pl.multiple_of(at * block, block), block)
        return pltpu.make_async_copy(src, xbuf.at[:, lanes], xsem.at[at])

    def w_copy(src, at, part):
        row = pl.multiple_of(at * block + part * half, half)
        return pltpu.make_async_copy(src, wbuf.at[pl.ds(row, half)], wsem.at[at * 2 + part])

    def needed(at, part):
        dist = (at // 2) ^ s
        kind = jnp.where(at % 2 == c, 0, 2) + jnp.where(part == g, 0, 1)
        have = dist == 0
        for d, k in EARLY_PIECES:
            have = have | ((dist == d) & (kind == k))
        fresh = (at // near == h) | (at - (1 - h) * near < far_early)
        return (have & fresh) != last

    if last:
        pltpu.make_async_copy(acc_in, acc, asem).start()
    else:
        acc[...] = jnp.zeros_like(acc)
    for part in range(2):
        for core, src in ((c, own), (1 - c, sib)):

            @pl.when(needed(s * 2 + core, part))
            def _():
                w_copy(src.at[pl.ds(part * half, half)], s * 2 + core, part).start()

    for i in range(near):
        x_copy(x_own.at[:, i * block : (i + 1) * block], h * near + i).start()
    at = (1 - h) * near
    for x_far, width in zip(xs, widths):
        for i in range(width):
            x_copy(x_far.at[:, i * block : (i + 1) * block], at).start()
            at = at + 1
    for (d, k), src in pieces.items():
        core = c if k < 2 else 1 - c
        part = g if k % 2 == 0 else 1 - g

        @pl.when(needed((s ^ d) * 2 + core, part))
        def _():
            w_copy(src, (s ^ d) * 2 + core, part).start()

    if last:
        pltpu.make_async_copy(acc_in, acc, asem).wait()

    @pl.loop(0, blocks)
    def _(n):
        at = lax.rem(n + h * near, blocks)

        @pl.when((n < near) | (n - near < sum(widths)))
        def _():
            x_copy(x_own.at[:, :block], at).wait()

        @pl.loop(0, 2)
        def _(part):
            @pl.when(needed(at, part))
            def _():
                w_copy(own.at[pl.ds(0, half)], at, part).wait()
                off = pl.multiple_of(at * block + part * half, half)
                acc[...] += jnp.dot(
                    xbuf[:, pl.ds(off, half)],
                    wbuf[pl.ds(off, half), :],
                    preferred_element_type=jnp.float32,
                )

    if last:
        out_ref[...] = acc[...].astype(out_ref.dtype)


def project(x, xs, own, sib, pieces, acc=None):
    last = acc is not None
    tokens, feats = x.shape
    block, width = own.shape
    near = feats // block
    widths = [v.shape[1] // block for v in xs]
    given = [pieces[name] for name in (ALL_PIECES if last else EARLY_PIECES)]
    anywhere = pl.BlockSpec(memory_space=pl.ANY)
    args = [x, *xs, own, sib, *given] + ([acc] if last else [])
    scratch = [
        pltpu.VMEM((tokens, 2 * feats), x.dtype),
        pltpu.VMEM((2 * feats, width), x.dtype),
        pltpu.SemaphoreType.DMA((2 * near,)),
        pltpu.SemaphoreType.DMA((4 * near,)),
    ]
    if last:
        scratch += [pltpu.VMEM((tokens, width), jnp.float32), pltpu.SemaphoreType.DMA]
    return pl.pallas_call(
        functools.partial(project_kernel, near, widths, last),
        out_shape=jax.ShapeDtypeStruct((tokens, width), jnp.bfloat16 if last else jnp.float32),
        in_specs=[anywhere] * len(args),
        out_specs=pl.BlockSpec(memory_space=pltpu.VMEM),
        scratch_shapes=scratch,
        compiler_params=pltpu.CompilerParams(vmem_limit_bytes=56 << 20),
        cost_estimate=pl.CostEstimate(
            flops=2 * tokens * feats * width, bytes_accessed=16 << 20, transcendentals=0
        ),
    )(*args)


def gathered_projection(x, own, wanted):
    g, s = lax.axis_index("groups"), lax.axis_index("seq")
    inner = (s == 1) | (s == 2)
    block = own.shape[0]
    tie = lax.optimization_barrier

    def sub(value):
        return lax.ppermute(value, "sub", SWAP)

    def across(value):
        return lax.ppermute(value, "groups", SWAP)

    def along(value, *pairs):
        return lax.ppermute(value, "seq", pairs)

    def far(value):
        return lax.ppermute(value, "head", SWAP)

    unit = lax.dynamic_slice_in_dim(own, g * (block // 2), block // 2, axis=0)
    x0, x1 = far(x[:, :block]), far(x[:, block : 2 * block])
    one = along(unit, (0, 1), (1, 0), (2, 3), (3, 2))
    mid = along(unit, (1, 2), (2, 1))
    one, mid, x0, x_rest, own_later = tie((one, mid, x0, x[:, 2 * block :], own))
    mid_two = along(one, (1, 2), (2, 1))
    out_two = along(mid, (1, 0), (2, 3))
    moved = {(1, 0): one, (1, 1): across(one), (1, 2): sub(one)}
    x2 = far(x_rest)
    mid_two, out_two, x1, moved[1, 1], own_later = tie(
        (mid_two, out_two, x1, moved[1, 1], own_later)
    )
    two = jnp.where(inner, mid_two, out_two)
    out_three = along(mid_two, (1, 0), (2, 3))
    moved.update({(2, 0): two, (2, 1): across(two), (2, 2): sub(two), (1, 3): sub(moved[1, 1])})
    sib = sub(own_later)
    out_three, moved[2, 2], moved[1, 3], sib, wanted = tie(
        (out_three, moved[2, 2], moved[1, 3], sib, wanted)
    )
    three = jnp.where(inner, mid, out_three)
    moved.update({(3, 0): three, (3, 1): across(three), (3, 2): sub(three), (2, 3): sub(moved[2, 1])})
    lists = jnp.stack([wanted] + [lax.ppermute(wanted, "seq", xor(4, d)) for d in (1, 2, 3)])
    twin_lists = sub(lists)
    acc = project(x, [x0, x1], own, sib, moved)
    moved[3, 3] = sub(moved[3, 1])
    return project(x, [x0, x1, x2], own, sib, moved, acc), lists, twin_lists


def plain_projection(x, own):
    head = lax.axis_size("head")
    feats = x.shape[1]
    weights = lax.all_gather(own, ("seq", "sub"), axis=0, tiled=True)
    sums = None
    for d in range(head):
        rows = x if d == 0 else lax.ppermute(x, "head", rotation(head, -d))
        at = lax.rem(lax.axis_index("head") + d, head) * feats
        term = jnp.dot(
            rows,
            lax.dynamic_slice_in_dim(weights, at, feats, axis=0),
            preferred_element_type=jnp.float32,
        )
        sums = term if sums is None else sums + term
    return sums.astype(jnp.bfloat16)


def spread(order, tokens, share, slot):
    place = lax.iota(jnp.int32, tokens)
    block = slot // tokens
    before = (block[None, :] == block[:, None]) & (place[None, :] < place[:, None])
    position = order(block) * share + jnp.sum(before.astype(jnp.int32), axis=1)
    hits = position[:, None] == place[None, :]
    wanted = jnp.sum(jnp.where(hits, (slot - block * tokens)[:, None], 0), axis=0)
    return hits.astype(jnp.bfloat16), wanted


def selected(asked, rows):
    pick = (asked[:, None] == lax.iota(jnp.int32, rows.shape[0])[None, :]).astype(jnp.bfloat16)
    return jnp.dot(pick, rows, preferred_element_type=jnp.float32).astype(jnp.bfloat16)


def local_moments(both, heads, dim):
    keys = both[:, : heads * dim].reshape(both.shape[0], heads, dim)
    return jnp.einsum("thi,thj->hij", keys, keys, preferred_element_type=jnp.float32)


def core_split(values, c):
    keep = lax.dynamic_index_in_dim(values, c, 0, keepdims=False)
    give = lax.dynamic_index_in_dim(values, 1 - c, 0, keepdims=False)
    return keep + lax.ppermute(give, "sub", SWAP)


def per_device(hidden_states, key_w, value_w, basis, slot):
    tokens = hidden_states.shape[0]
    seq, head, cores = lax.axis_size("seq"), lax.axis_size("head"), lax.axis_size("sub")
    s, c = lax.axis_index("seq"), lax.axis_index("sub")
    peers = seq * cores
    share = tokens // peers
    heads, dim, rank = basis.shape
    mine = heads // cores
    width = heads * dim
    own = jnp.concatenate([key_w, value_w], axis=1)
    basis_here = lax.dynamic_slice_in_dim(basis, c * mine, mine, axis=0)

    if seq == 4 and head == 2 and lax.axis_size("groups") == 2 and mine == 2:
        unpick, wanted = spread(lambda b: b ^ (s * cores + c), tokens, share, slot)
        both, lists, twin_lists = gathered_projection(hidden_states, own, wanted)
        packed = pack(local_moments(both, heads, dim).reshape(cores, mine, dim, dim))
        chip = core_split(packed, c)
        parts = [chip] + [lax.ppermute(chip, "seq", xor(seq, d)) for d in (1, 2, 3)]
        near = [lists[d, 2 * d * share : (2 * d + 1) * share] for d in range(seq)]
        twin = [twin_lists[d, (2 * d + 1) * share : (2 * d + 2) * share] for d in range(seq)]
        give = selected(jnp.concatenate(twin), both)
        keep = selected(jnp.concatenate(near), both)
        taken = lax.ppermute(give, "sub", SWAP)
        pairs = jnp.stack(
            [v.reshape(seq, share, 2 * width) for v in (keep, taken)], axis=1
        ).reshape(seq, cores * share, 2 * width)
        got = jnp.concatenate(
            [pairs[0]] + [lax.ppermute(pairs[d], "seq", xor(seq, d)) for d in (1, 2, 3)]
        )
    else:
        unpick, wanted = spread(lambda b: b, tokens, share, slot)
        asked = lax.all_to_all(wanted, ("seq", "sub"), split_axis=0, concat_axis=0, tiled=True)
        both = plain_projection(hidden_states, own)
        chip = core_split(local_moments(both, heads, dim).reshape(cores, mine, dim, dim), c)
        parts = [lax.psum(chip, "seq")]
        got = lax.all_to_all(
            selected(asked, both), ("seq", "sub"), split_axis=0, concat_axis=0, tiled=True
        )

    solved = solve(parts, basis_here, tokens * peers)
    other = lax.ppermute(solved, "sub", SWAP)
    maps = jnp.where(c == 0, jnp.concatenate([solved, other]), jnp.concatenate([other, solved]))
    rows = jnp.dot(unpick, got, preferred_element_type=jnp.float32).astype(jnp.bfloat16)
    coeffs = jnp.einsum(
        "thd,hdr->thr",
        rows[:, :width].astype(jnp.float32).reshape(tokens, heads, dim),
        maps,
        precision=lax.Precision.HIGHEST,
    )
    return coeffs.reshape(tokens, heads * rank).astype(jnp.bfloat16), rows[:, width:]


def solution(mesh):
    return jax.shard_map(
        per_device,
        mesh=mesh,
        in_specs=(
            P(("groups", "seq", "sub"), "head"),
            P(("seq", "sub"), "head"),
            P(("seq", "sub"), "head"),
            P("head", None, None),
            P(("groups", "seq", "sub")),
        ),
        out_specs=(P(("groups", "seq", "sub"), "head"), P(("groups", "seq", "sub"), "head")),
        check_vma=False,
    )
```

```python
import functools

import jax
import jax.numpy as jnp
from jax import lax
from jax.experimental import pallas as pl
from jax.experimental.pallas import tpu as pltpu
from jax.sharding import PartitionSpec as P

ridge_share = 0.05
SWAP = [(0, 1), (1, 0)]


def rotation(count, shift):
    return [(i, (i + shift) % count) for i in range(count)]


def xor(count, distance):
    return [(i, i ^ distance) for i in range(count)]


def pack(moments):
    first, second = moments[..., 0, :, :], moments[..., 1, :, :]
    dim = first.shape[-1]
    row = lax.broadcasted_iota(jnp.int32, (dim, dim), 0)
    col = lax.broadcasted_iota(jnp.int32, (dim, dim), 1)
    both = jnp.where(row >= col, first, second)
    diagonal = jnp.sum(jnp.where(row == col, second, 0.0), axis=-2, keepdims=True)
    return jnp.concatenate([both, jnp.broadcast_to(diagonal, (*both.shape[:-2], 8, dim))], axis=-2)


def unpack(packed):
    dim = packed.shape[1]
    row = lax.broadcasted_iota(jnp.int32, (dim, dim), 0)
    col = lax.broadcasted_iota(jnp.int32, (dim, dim), 1)
    both, diagonal = packed[:dim], packed[dim : dim + 1]
    turned = both.T
    first = jnp.where(row >= col, both, turned)
    second = jnp.where(row < col, both, jnp.where(row == col, diagonal, turned))
    return jnp.stack([first, second])


def solve_kernel(scale, parts, packed, *refs):
    m_refs, basis_ref, out_ref = refs[:parts], refs[parts], refs[parts + 1]
    heads, dim, _ = basis_ref.shape
    total = m_refs[0][...]
    for ref in m_refs[1:]:
        total = total + ref[...]
    total = total * scale
    if packed:
        total = unpack(total)
    row = lax.broadcasted_iota(jnp.int32, (1, dim, dim), 1)
    col = lax.broadcasted_iota(jnp.int32, (1, dim, dim), 2)
    diag = row == col
    trace = jnp.sum(jnp.where(diag, total, 0.0), axis=(1, 2), keepdims=True)
    work = total + jnp.where(diag, ridge_share * trace / dim, 0.0)
    tiles = [work[:, r : r + 8, :] for r in range(0, dim, 8)]
    lane = lax.broadcasted_iota(jnp.int32, (1, 1, dim), 2)
    sub = lax.broadcasted_iota(jnp.int32, (1, 8, 1), 1)
    for j in range(dim):
        t0, j0 = j // 8, j % 8
        pivot_row = tiles[t0][:, j0 : j0 + 1, :]
        inv = 1.0 / pivot_row[:, :, j : j + 1]
        scaled = jnp.where(lane == j, inv, pivot_row * inv)
        at = lane == j
        for t in range(t0, dim // 8):
            if t == t0 and j0 == 7:
                continue
            f = tiles[t][:, :, j : j + 1]
            if t == t0:
                f = jnp.where(sub > j0, f, 0.0)
                base = jnp.where(at & (sub > j0), 0.0, tiles[t])
            else:
                base = jnp.where(at, 0.0, tiles[t])
            tiles[t] = base - f * scaled
    work = jnp.concatenate(tiles, axis=1)
    pivots = jnp.sum(jnp.where(diag, work, 0.0), axis=2, keepdims=True)
    inverse = jnp.where(row > col, work, jnp.where(diag, 1.0, 0.0))
    scaled_basis = basis_ref[...] * lax.rsqrt(pivots)
    for h in range(heads):
        out_ref[h] = lax.dot_general(
            inverse[h].T,
            scaled_basis[h],
            (((1,), (0,)), ((), ())),
            precision=lax.Precision.HIGHEST,
            preferred_element_type=jnp.float32,
        )


def solve(parts, basis, token_total):
    heads, dim, rank = basis.shape
    vmem = pl.BlockSpec(memory_space=pltpu.VMEM)
    return pl.pallas_call(
        functools.partial(solve_kernel, 1.0 / token_total, len(parts), parts[0].ndim == 2),
        out_shape=jax.ShapeDtypeStruct((heads, dim, rank), jnp.float32),
        in_specs=[vmem] * (len(parts) + 1),
        out_specs=vmem,
        cost_estimate=pl.CostEstimate(flops=heads * dim**3, bytes_accessed=4 * heads * dim * dim, transcendentals=0),
    )(*parts, basis)


ALL_PIECES = [(d, k) for d in (1, 2, 3) for k in range(4)]
EARLY_PIECES = [(1, 0), (1, 1), (1, 2), (1, 3), (2, 0), (2, 2), (3, 0)]


def project_kernel(near, widths, last, *refs):
    refs = list(refs)
    x_own, xs = refs.pop(0), [refs.pop(0) for _ in widths]
    own, sib = refs.pop(0), refs.pop(0)
    pieces = {name: refs.pop(0) for name in (ALL_PIECES if last else EARLY_PIECES)}
    if last:
        acc_in, out_ref, xbuf, wbuf, xsem, wsem, acc, asem = refs
    else:
        acc, xbuf, wbuf, xsem, wsem = refs
    g, s, h, c = (lax.axis_index(a) for a in ("groups", "seq", "head", "sub"))
    block = own.shape[0]
    half = block // 2
    count = 2 * near
    far_early = sum(widths) - (widths[-1] if last else 0)

    def x_copy(src, n):
        lanes = pl.ds(pl.multiple_of(n * half, half), half)
        return pltpu.make_async_copy(src, xbuf.at[:, lanes], xsem.at[n])

    def w_copy(src, n):
        return pltpu.make_async_copy(src, wbuf.at[pl.ds(pl.multiple_of(n * half, half), half)], wsem.at[n])

    def needed(n):
        dist = (n // 4) ^ s
        kind = jnp.where((n // 2) % 2 == c, 0, 2) + jnp.where(n % 2 == g, 0, 1)
        have = dist == 0
        for d, k in EARLY_PIECES:
            have = have | ((dist == d) & (kind == k))
        fresh = (n // near == h) | (n - (1 - h) * near < far_early)
        return (have & fresh) != last

    if last:
        pltpu.make_async_copy(acc_in, acc, asem).start()
    else:
        acc[...] = jnp.zeros_like(acc)
    for i in range(near):
        x_copy(x_own.at[:, i * half : (i + 1) * half], h * near + i).start()
    for part in range(2):
        for core, src in ((c, own), (1 - c, sib)):
            n = s * 4 + core * 2 + part

            @pl.when(needed(n))
            def _():
                w_copy(src.at[pl.ds(part * half, half)], n).start()

    for (d, k), src in pieces.items():
        core = c if k < 2 else 1 - c
        n = (s ^ d) * 4 + core * 2 + (g if k % 2 == 0 else 1 - g)

        @pl.when(needed(n))
        def _():
            w_copy(src, n).start()

    n = (1 - h) * near
    for x_far, width in zip(xs, widths):
        for i in range(width):
            x_copy(x_far.at[:, i * half : (i + 1) * half], n).start()
            n = n + 1
    if last:
        pltpu.make_async_copy(acc_in, acc, asem).wait()

    @pl.loop(0, near + sum(widths))
    def _(i):
        n = lax.rem(i + h * near, count)
        x_copy(x_own.at[:, :half], n).wait()

        @pl.when(needed(n))
        def _():
            w_copy(own.at[pl.ds(0, half)], n).wait()
            off = pl.multiple_of(n * half, half)
            acc[...] += jnp.dot(
                xbuf[:, pl.ds(off, half)],
                wbuf[pl.ds(off, half), :],
                preferred_element_type=jnp.float32,
            )

    if last:
        out_ref[...] = acc[...].astype(out_ref.dtype)


def project(x, xs, own, sib, pieces, acc=None):
    last = acc is not None
    tokens, feats = x.shape
    block, width = own.shape
    near = 2 * feats // block
    widths = [2 * v.shape[1] // block for v in xs]
    given = [pieces[name] for name in (ALL_PIECES if last else EARLY_PIECES)]
    anywhere = pl.BlockSpec(memory_space=pl.ANY)
    args = [x, *xs, own, sib, *given] + ([acc] if last else [])
    scratch = [
        pltpu.VMEM((tokens, 2 * feats), x.dtype),
        pltpu.VMEM((2 * feats, width), x.dtype),
        pltpu.SemaphoreType.DMA((2 * near,)),
        pltpu.SemaphoreType.DMA((2 * near,)),
    ]
    if last:
        scratch += [pltpu.VMEM((tokens, width), jnp.float32), pltpu.SemaphoreType.DMA]
    return pl.pallas_call(
        functools.partial(project_kernel, near, widths, last),
        out_shape=jax.ShapeDtypeStruct((tokens, width), jnp.bfloat16 if last else jnp.float32),
        in_specs=[anywhere] * len(args),
        out_specs=pl.BlockSpec(memory_space=pltpu.VMEM),
        scratch_shapes=scratch,
        compiler_params=pltpu.CompilerParams(vmem_limit_bytes=36 << 20),
        cost_estimate=pl.CostEstimate(
            flops=2 * tokens * feats * width, bytes_accessed=16 << 20, transcendentals=0
        ),
    )(*args)


def gathered_projection(x, own, wanted):
    g, s = lax.axis_index("groups"), lax.axis_index("seq")
    inner = (s == 1) | (s == 2)
    block, feats = own.shape[0], x.shape[1]
    tie = lax.optimization_barrier

    def sub(value):
        return lax.ppermute(value, "sub", SWAP)

    def across(value):
        return lax.ppermute(value, "groups", SWAP)

    def along(value, *pairs):
        return lax.ppermute(value, "seq", pairs)

    def far(value):
        return lax.ppermute(value, "head", SWAP)

    unit = lax.dynamic_slice_in_dim(own, g * (block // 2), block // 2, axis=0)
    bounds = [0, 2, 4, 6, 8]

    def part(value, i):
        return value[:, bounds[i] * feats // 8 : bounds[i + 1] * feats // 8]

    x0 = far(part(x, 0))
    one = along(unit, (0, 1), (1, 0), (2, 3), (3, 2))
    mid = along(unit, (1, 2), (2, 1))
    x1 = far(part(tie(x), 1))
    one, mid, x_a = tie((one, mid, x))
    third = part(x_a, 2)
    mid_two = along(one, (1, 2), (2, 1))
    out_two = along(mid, (1, 0), (2, 3))
    one_twin = across(one)
    mid_two, out_two, x0, x1, one_twin, third, one_b, x_b = tie(
        (mid_two, out_two, x0, x1, one_twin, third, one, x)
    )
    two = jnp.where(inner, mid_two, out_two)
    two, mid_two = tie((two, mid_two))
    out_three = along(mid_two, (1, 0), (2, 3))
    x2 = far(third)
    two_twin = across(two)
    fourth = part(x_b, 3)
    one_sib, one_twin_sib = sub(one_b), sub(one_twin)
    one_sib, one_twin_sib, own_b, two_b = tie((one_sib, one_twin_sib, own, two))
    sib, two_sib = sub(own_b), sub(two_b)
    out_three, x2, two_twin, sib, two_sib, fourth = tie(
        (out_three, x2, two_twin, sib, two_sib, fourth)
    )
    three = jnp.where(inner, mid, out_three)
    twin = across(three)
    x3 = far(fourth)
    moved = {(1, 0): one, (1, 1): one_twin, (1, 2): one_sib, (1, 3): one_twin_sib}
    moved.update({(2, 0): two, (2, 2): two_sib, (3, 0): three})
    acc = project(x, [x0, x1, x2], own, sib, moved)
    moved.update({(2, 1): two_twin, (2, 3): sub(two_twin), (3, 2): sub(three)})
    acc, wanted = tie((acc, wanted))
    lists = jnp.stack([wanted] + [lax.ppermute(wanted, "seq", xor(4, d)) for d in (1, 2, 3)])
    twin_lists = sub(lists)
    twin, x3 = tie((twin, x3))
    moved.update({(3, 1): twin, (3, 3): sub(twin)})
    return project(x, [x0, x1, x2, x3], own, sib, moved, acc), lists, twin_lists


def plain_projection(x, own):
    head = lax.axis_size("head")
    feats = x.shape[1]
    weights = lax.all_gather(own, ("seq", "sub"), axis=0, tiled=True)
    sums = None
    for d in range(head):
        rows = x if d == 0 else lax.ppermute(x, "head", rotation(head, -d))
        at = lax.rem(lax.axis_index("head") + d, head) * feats
        term = jnp.dot(
            rows,
            lax.dynamic_slice_in_dim(weights, at, feats, axis=0),
            preferred_element_type=jnp.float32,
        )
        sums = term if sums is None else sums + term
    return sums.astype(jnp.bfloat16)


def spread(order, tokens, share, slot):
    place = lax.iota(jnp.int32, tokens)
    block = slot // tokens
    before = (block[None, :] == block[:, None]) & (place[None, :] < place[:, None])
    position = order(block) * share + jnp.sum(before.astype(jnp.int32), axis=1)
    hits = position[:, None] == place[None, :]
    wanted = jnp.sum(jnp.where(hits, (slot - block * tokens)[:, None], 0), axis=0)
    return hits.astype(jnp.bfloat16), wanted


def selected(asked, rows):
    pick = (asked[:, None] == lax.iota(jnp.int32, rows.shape[0])[None, :]).astype(jnp.bfloat16)
    return jnp.dot(pick, rows, preferred_element_type=jnp.float32).astype(jnp.bfloat16)


def local_moments(both, heads, dim):
    keys = both[:, : heads * dim].reshape(both.shape[0], heads, dim)
    return jnp.einsum("thi,thj->hij", keys, keys, preferred_element_type=jnp.float32)


def core_split(values, c):
    keep = lax.dynamic_index_in_dim(values, c, 0, keepdims=False)
    give = lax.dynamic_index_in_dim(values, 1 - c, 0, keepdims=False)
    return keep + lax.ppermute(give, "sub", SWAP)


def per_device(hidden_states, key_w, value_w, basis, slot):
    tokens = hidden_states.shape[0]
    seq, head, cores = lax.axis_size("seq"), lax.axis_size("head"), lax.axis_size("sub")
    s, c = lax.axis_index("seq"), lax.axis_index("sub")
    peers = seq * cores
    share = tokens // peers
    heads, dim, rank = basis.shape
    mine = heads // cores
    width = heads * dim
    own = jnp.concatenate([key_w, value_w], axis=1)
    basis_here = lax.dynamic_slice_in_dim(basis, c * mine, mine, axis=0)

    if seq == 4 and head == 2 and lax.axis_size("groups") == 2 and mine == 2:
        unpick, wanted = spread(lambda b: b ^ (s * cores + c), tokens, share, slot)
        both, lists, twin_lists = gathered_projection(hidden_states, own, wanted)
        packed = pack(local_moments(both, heads, dim).reshape(cores, mine, dim, dim))
        chip = core_split(packed, c)
        near = [lists[d, 2 * d * share : (2 * d + 1) * share] for d in range(seq)]
        twin = [twin_lists[d, (2 * d + 1) * share : (2 * d + 2) * share] for d in range(seq)]
        give = selected(jnp.concatenate(twin), both)
        keep = selected(jnp.concatenate(near), both)
        taken = lax.ppermute(give, "sub", SWAP)
        parts = [chip] + [lax.ppermute(chip, "seq", xor(seq, d)) for d in (1, 2, 3)]
        keep, taken, *parts = lax.optimization_barrier((keep, taken, *parts))
        pairs = jnp.stack(
            [v.reshape(seq, share, 2 * width) for v in (keep, taken)], axis=1
        ).reshape(seq, cores * share, 2 * width)
        got = jnp.concatenate(
            [pairs[0]] + [lax.ppermute(pairs[d], "seq", xor(seq, d)) for d in (1, 2, 3)]
        )
    else:
        unpick, wanted = spread(lambda b: b, tokens, share, slot)
        asked = lax.all_to_all(wanted, ("seq", "sub"), split_axis=0, concat_axis=0, tiled=True)
        both = plain_projection(hidden_states, own)
        chip = core_split(local_moments(both, heads, dim).reshape(cores, mine, dim, dim), c)
        parts = [lax.psum(chip, "seq")]
        got = lax.all_to_all(
            selected(asked, both), ("seq", "sub"), split_axis=0, concat_axis=0, tiled=True
        )

    solved = solve(parts, basis_here, tokens * peers)
    other = lax.ppermute(solved, "sub", SWAP)
    maps = jnp.where(c == 0, jnp.concatenate([solved, other]), jnp.concatenate([other, solved]))
    rows = jnp.dot(unpick, got, preferred_element_type=jnp.float32).astype(jnp.bfloat16)
    coeffs = jnp.einsum(
        "thd,hdr->thr",
        rows[:, :width].astype(jnp.float32).reshape(tokens, heads, dim),
        maps,
        precision=lax.Precision.HIGHEST,
    )
    return coeffs.reshape(tokens, heads * rank).astype(jnp.bfloat16), rows[:, width:]


def solution(mesh):
    return jax.shard_map(
        per_device,
        mesh=mesh,
        in_specs=(
            P(("groups", "seq", "sub"), "head"),
            P(("seq", "sub"), "head"),
            P(("seq", "sub"), "head"),
            P("head", None, None),
            P(("groups", "seq", "sub")),
        ),
        out_specs=(P(("groups", "seq", "sub"), "head"), P(("groups", "seq", "sub"), "head")),
        check_vma=False,
    )
```

```python
import functools

import jax
import jax.numpy as jnp
from jax import lax
from jax.experimental import pallas as pl
from jax.experimental.pallas import tpu as pltpu
from jax.sharding import PartitionSpec as P

ridge_share = 0.05
SWAP = [(0, 1), (1, 0)]


def rotation(count, shift):
    return [(i, (i + shift) % count) for i in range(count)]


def xor(count, distance):
    return [(i, i ^ distance) for i in range(count)]


def pack(moments):
    first, second = moments[..., 0, :, :], moments[..., 1, :, :]
    dim = first.shape[-1]
    row = lax.broadcasted_iota(jnp.int32, (dim, dim), 0)
    col = lax.broadcasted_iota(jnp.int32, (dim, dim), 1)
    both = jnp.where(row >= col, first, second)
    diagonal = jnp.sum(jnp.where(row == col, second, 0.0), axis=-2, keepdims=True)
    return jnp.concatenate([both, jnp.broadcast_to(diagonal, (*both.shape[:-2], 8, dim))], axis=-2)


def unpack(packed):
    dim = packed.shape[1]
    row = lax.broadcasted_iota(jnp.int32, (dim, dim), 0)
    col = lax.broadcasted_iota(jnp.int32, (dim, dim), 1)
    both, diagonal = packed[:dim], packed[dim : dim + 1]
    turned = both.T
    first = jnp.where(row >= col, both, turned)
    second = jnp.where(row < col, both, jnp.where(row == col, diagonal, turned))
    return jnp.stack([first, second])


def solve_kernel(scale, parts, packed, *refs):
    m_refs, basis_ref, out_ref = refs[:parts], refs[parts], refs[parts + 1]
    heads, dim, _ = basis_ref.shape
    total = m_refs[0][...]
    for ref in m_refs[1:]:
        total = total + ref[...]
    total = total * scale
    if packed:
        total = unpack(total)
    row = lax.broadcasted_iota(jnp.int32, (1, dim, dim), 1)
    col = lax.broadcasted_iota(jnp.int32, (1, dim, dim), 2)
    diag = row == col
    trace = jnp.sum(jnp.where(diag, total, 0.0), axis=(1, 2), keepdims=True)
    work = total + jnp.where(diag, ridge_share * trace / dim, 0.0)
    tiles = [work[:, r : r + 8, :] for r in range(0, dim, 8)]
    lane = lax.broadcasted_iota(jnp.int32, (1, 1, dim), 2)
    sub = lax.broadcasted_iota(jnp.int32, (1, 8, 1), 1)
    for j in range(dim):
        t0, j0 = j // 8, j % 8
        pivot_row = tiles[t0][:, j0 : j0 + 1, :]
        inv = 1.0 / pivot_row[:, :, j : j + 1]
        scaled = jnp.where(lane == j, inv, pivot_row * inv)
        at = lane == j
        for t in range(t0, dim // 8):
            if t == t0 and j0 == 7:
                continue
            f = tiles[t][:, :, j : j + 1]
            if t == t0:
                f = jnp.where(sub > j0, f, 0.0)
                base = jnp.where(at & (sub > j0), 0.0, tiles[t])
            else:
                base = jnp.where(at, 0.0, tiles[t])
            tiles[t] = base - f * scaled
    work = jnp.concatenate(tiles, axis=1)
    pivots = jnp.sum(jnp.where(diag, work, 0.0), axis=2, keepdims=True)
    inverse = jnp.where(row > col, work, jnp.where(diag, 1.0, 0.0))
    scaled_basis = basis_ref[...] * lax.rsqrt(pivots)
    for h in range(heads):
        out_ref[h] = lax.dot_general(
            inverse[h].T,
            scaled_basis[h],
            (((1,), (0,)), ((), ())),
            precision=lax.Precision.HIGHEST,
            preferred_element_type=jnp.float32,
        )


def solve(parts, basis, token_total):
    heads, dim, rank = basis.shape
    vmem = pl.BlockSpec(memory_space=pltpu.VMEM)
    return pl.pallas_call(
        functools.partial(solve_kernel, 1.0 / token_total, len(parts), parts[0].ndim == 2),
        out_shape=jax.ShapeDtypeStruct((heads, dim, rank), jnp.float32),
        in_specs=[vmem] * (len(parts) + 1),
        out_specs=vmem,
        cost_estimate=pl.CostEstimate(flops=6000 * heads * dim**3 // 2, bytes_accessed=4 * heads * dim * dim, transcendentals=0),
    )(*parts, basis)


ALL_PIECES = [(d, k) for d in (1, 2, 3) for k in range(4)]
EARLY_PIECES = [(1, 0), (1, 1), (1, 2), (1, 3), (2, 0), (2, 1), (2, 2), (2, 3), (3, 0), (3, 2)]


def project_kernel(near, widths, last, *refs):
    refs = list(refs)
    x_own, xs = refs.pop(0), [refs.pop(0) for _ in widths]
    own, sib = refs.pop(0), refs.pop(0)
    pieces = {name: refs.pop(0) for name in (ALL_PIECES if last else EARLY_PIECES)}
    if last:
        acc_in, out_ref, xbuf, wbuf, xsem, wsem, acc = refs
    else:
        acc, xbuf, wbuf, xsem, wsem = refs
    g, s, h, c = (lax.axis_index(a) for a in ("groups", "seq", "head", "sub"))
    block = own.shape[0]
    half = block // 2
    count = 2 * near
    far_early = sum(widths) - (widths[-1] if last else 0)

    def x_copy(src, n):
        lanes = pl.ds(pl.multiple_of(n * half, half), half)
        return pltpu.make_async_copy(src, xbuf.at[:, lanes], xsem.at[n])

    def w_copy(src, n):
        return pltpu.make_async_copy(src, wbuf.at[pl.ds(pl.multiple_of(n * half, half), half)], wsem.at[n])

    def needed(n):
        dist = (n // 4) ^ s
        kind = jnp.where((n // 2) % 2 == c, 0, 2) + jnp.where(n % 2 == g, 0, 1)
        have = dist == 0
        for d, k in EARLY_PIECES:
            have = have | ((dist == d) & (kind == k))
        fresh = (n // near == h) | (n - (1 - h) * near < far_early)
        return (have & fresh) != last

    for i in range(near):
        x_copy(x_own.at[:, i * half : (i + 1) * half], h * near + i).start()
    for part in range(2):
        for core, src in ((c, own), (1 - c, sib)):
            n = s * 4 + core * 2 + part

            @pl.when(needed(n))
            def _():
                w_copy(src.at[pl.ds(part * half, half)], n).start()

    for (d, k), src in pieces.items():
        core = c if k < 2 else 1 - c
        n = (s ^ d) * 4 + core * 2 + (g if k % 2 == 0 else 1 - g)

        @pl.when(needed(n))
        def _():
            w_copy(src, n).start()

    n = (1 - h) * near
    for x_far, width in zip(xs, widths):
        for i in range(width):
            x_copy(x_far.at[:, i * half : (i + 1) * half], n).start()
            n = n + 1
    acc[...] = acc_in[...] if last else jnp.zeros_like(acc)

    @pl.loop(0, near + sum(widths))
    def _(i):
        n = lax.rem(i + h * near, count)
        x_copy(x_own.at[:, :half], n).wait()

        @pl.when(needed(n))
        def _():
            w_copy(own.at[pl.ds(0, half)], n).wait()
            off = pl.multiple_of(n * half, half)
            acc[...] += jnp.dot(
                xbuf[:, pl.ds(off, half)],
                wbuf[pl.ds(off, half), :],
                preferred_element_type=jnp.float32,
            )

    if last:
        out_ref[...] = acc[...].astype(out_ref.dtype)


def project(x, xs, own, sib, pieces, acc=None):
    last = acc is not None
    tokens, feats = x.shape
    block, width = own.shape
    near = 2 * feats // block
    widths = [2 * v.shape[1] // block for v in xs]
    given = [pieces[name] for name in (ALL_PIECES if last else EARLY_PIECES)]
    hbm, vmem = pl.BlockSpec(memory_space=pltpu.HBM), pl.BlockSpec(memory_space=pltpu.VMEM)
    args = [pltpu.with_memory_space_constraint(v, pltpu.HBM) for v in (x, *xs, own, sib, *given)]
    specs = [hbm] * len(args)
    scratch = [
        pltpu.VMEM((tokens, 2 * feats), x.dtype),
        pltpu.VMEM((2 * feats, width), x.dtype),
        pltpu.SemaphoreType.DMA((2 * near,)),
        pltpu.SemaphoreType.DMA((2 * near,)),
    ]
    if last:
        args.append(acc)
        specs.append(vmem)
        scratch.append(pltpu.VMEM((tokens, width), jnp.float32))
    return pl.pallas_call(
        functools.partial(project_kernel, near, widths, last),
        out_shape=jax.ShapeDtypeStruct((tokens, width), jnp.bfloat16 if last else jnp.float32),
        in_specs=specs,
        out_specs=vmem,
        scratch_shapes=scratch,
        compiler_params=pltpu.CompilerParams(vmem_limit_bytes=36 << 20),
        cost_estimate=pl.CostEstimate(
            flops=2 * tokens * feats * width, bytes_accessed=16 << 20, transcendentals=0
        ),
    )(*args)


def gathered_projection(x, own, wanted):
    g, s = lax.axis_index("groups"), lax.axis_index("seq")
    inner = (s == 1) | (s == 2)
    block, feats = own.shape[0], x.shape[1]
    tie = lax.optimization_barrier

    def sub(value):
        return lax.ppermute(value, "sub", SWAP)

    def across(value):
        return lax.ppermute(value, "groups", SWAP)

    def along(value, *pairs):
        return lax.ppermute(value, "seq", pairs)

    def far(value):
        return lax.ppermute(value, "head", SWAP)

    unit = lax.dynamic_slice_in_dim(own, g * (block // 2), block // 2, axis=0)
    bounds = [0, 2, 4, 6, 8]

    def part(value, i):
        return value[:, bounds[i] * feats // 8 : bounds[i + 1] * feats // 8]

    x0 = far(part(x, 0))
    one = along(unit, (0, 1), (1, 0), (2, 3), (3, 2))
    mid = along(unit, (1, 2), (2, 1))
    x1 = far(part(tie(x), 1))
    one, mid, x_a, sib = tie((one, mid, x, sub(own)))
    third = part(x_a, 2)
    mid_two = along(one, (1, 2), (2, 1))
    out_two = along(mid, (1, 0), (2, 3))
    one_twin = across(one)
    mid_two, out_two, x0, x1, one_twin, third, one_b, x_b = tie(
        (mid_two, out_two, x0, x1, one_twin, third, one, x)
    )
    two = jnp.where(inner, mid_two, out_two)
    two, mid_two = tie((two, mid_two))
    out_three = along(mid_two, (1, 0), (2, 3))
    x2 = far(third)
    two_twin = across(two)
    fourth = part(x_b, 3)
    one_sib, one_twin_sib = sub(one_b), sub(one_twin)
    out_three, x2, two_twin, one_sib, one_twin_sib, fourth, two_c = tie(
        (out_three, x2, two_twin, one_sib, one_twin_sib, fourth, two)
    )
    three = jnp.where(inner, mid, out_three)
    twin = across(three)
    x3 = far(fourth)
    moved = {(1, 0): one, (1, 1): one_twin, (1, 2): one_sib, (1, 3): one_twin_sib}
    moved.update({(2, 0): two, (2, 1): two_twin, (3, 0): three})
    moved.update({(2, 2): sub(two_c), (2, 3): sub(two_twin), (3, 2): sub(three)})
    acc = project(x, [x0, x1, x2], own, sib, moved)
    acc, wanted = tie((acc, wanted))
    lists = jnp.stack([wanted] + [lax.ppermute(wanted, "seq", xor(4, d)) for d in (1, 2, 3)])
    twin_lists = sub(lists)
    twin, x3, acc = tie((twin, x3, acc))
    moved.update({(3, 1): twin, (3, 3): sub(twin)})
    return project(x, [x0, x1, x2, x3], own, sib, moved, acc), lists, twin_lists


def plain_projection(x, own):
    head = lax.axis_size("head")
    feats = x.shape[1]
    weights = lax.all_gather(own, ("seq", "sub"), axis=0, tiled=True)
    sums = None
    for d in range(head):
        rows = x if d == 0 else lax.ppermute(x, "head", rotation(head, -d))
        at = lax.rem(lax.axis_index("head") + d, head) * feats
        term = jnp.dot(
            rows,
            lax.dynamic_slice_in_dim(weights, at, feats, axis=0),
            preferred_element_type=jnp.float32,
        )
        sums = term if sums is None else sums + term
    return sums.astype(jnp.bfloat16)


def finish_kernel(position_ref, mine_ref, other_ref, *refs):
    got, coeff_ref, value_ref = refs[:-2], refs[-2], refs[-1]
    rows = jnp.concatenate([r[...] for r in got])
    tokens, width = rows.shape
    half = width // 2
    heads, dim, rank = mine_ref.shape
    place = lax.broadcasted_iota(jnp.int32, (tokens, tokens), 1)
    unpick = (position_ref[...] == place).astype(jnp.bfloat16)
    rows = jnp.dot(unpick, rows, preferred_element_type=jnp.float32)
    value_ref[...] = rows[:, half:].astype(value_ref.dtype)
    first = lax.axis_index("sub") == 0
    maps = [jnp.where(first, mine_ref[i], other_ref[i]) for i in range(heads)]
    maps += [jnp.where(first, other_ref[i], mine_ref[i]) for i in range(heads)]
    coeffs = [
        jnp.dot(
            rows[:, i * dim : (i + 1) * dim],
            m,
            precision=lax.Precision.HIGHEST,
            preferred_element_type=jnp.float32,
        )
        for i, m in enumerate(maps)
    ]
    coeff_ref[...] = jnp.concatenate(coeffs, axis=1).astype(coeff_ref.dtype)


def finish(position, got, solved, other):
    heads, dim, rank = solved.shape
    tokens = position.shape[0]
    vmem = pl.BlockSpec(memory_space=pltpu.VMEM)
    return pl.pallas_call(
        finish_kernel,
        out_shape=(
            jax.ShapeDtypeStruct((tokens, 2 * heads * rank), jnp.bfloat16),
            jax.ShapeDtypeStruct((tokens, 2 * heads * dim), jnp.bfloat16),
        ),
        in_specs=[vmem] * (3 + len(got)),
        out_specs=(vmem, vmem),
        compiler_params=pltpu.CompilerParams(vmem_limit_bytes=24 << 20),
    )(position[:, None], solved, other, *got)


def spread(order, tokens, share, slot):
    place = lax.iota(jnp.int32, tokens)
    block = slot // tokens
    before = (block[None, :] == block[:, None]) & (place[None, :] < place[:, None])
    position = order(block) * share + jnp.sum(before.astype(jnp.int32), axis=1)
    hits = position[:, None] == place[None, :]
    wanted = jnp.sum(jnp.where(hits, (slot - block * tokens)[:, None], 0), axis=0)
    return position, wanted


def selected(asked, rows):
    pick = (asked[:, None] == lax.iota(jnp.int32, rows.shape[0])[None, :]).astype(jnp.bfloat16)
    return jnp.dot(pick, rows, preferred_element_type=jnp.float32).astype(jnp.bfloat16)


def local_moments(both, heads, dim):
    keys = both[:, : heads * dim].reshape(both.shape[0], heads, dim)
    return jnp.einsum("thi,thj->hij", keys, keys, preferred_element_type=jnp.float32)


def core_split(values, c):
    keep = lax.dynamic_index_in_dim(values, c, 0, keepdims=False)
    give = lax.dynamic_index_in_dim(values, 1 - c, 0, keepdims=False)
    return keep + lax.ppermute(give, "sub", SWAP)


def per_device(hidden_states, key_w, value_w, basis, slot):
    tokens = hidden_states.shape[0]
    seq, head, cores = lax.axis_size("seq"), lax.axis_size("head"), lax.axis_size("sub")
    s, c = lax.axis_index("seq"), lax.axis_index("sub")
    peers = seq * cores
    share = tokens // peers
    heads, dim, rank = basis.shape
    mine = heads // cores
    width = heads * dim
    own = jnp.concatenate([key_w, value_w], axis=1)
    basis_here = lax.dynamic_slice_in_dim(basis, c * mine, mine, axis=0)

    if seq == 4 and head == 2 and lax.axis_size("groups") == 2 and mine == 2:
        position, wanted = spread(lambda b: b ^ (s * cores + c), tokens, share, slot)
        both, lists, twin_lists = gathered_projection(hidden_states, own, wanted)
        packed = pack(local_moments(both, heads, dim).reshape(cores, mine, dim, dim))
        chip = core_split(packed, c)
        near = [lists[d, 2 * d * share : (2 * d + 1) * share] for d in range(seq)]
        twin = [twin_lists[d, (2 * d + 1) * share : (2 * d + 2) * share] for d in range(seq)]
        give = selected(jnp.concatenate(twin), both)
        keep = selected(jnp.concatenate(near), both)
        taken = lax.ppermute(give, "sub", SWAP)
        parts = [chip] + [lax.ppermute(chip, "seq", xor(seq, d)) for d in (1, 2, 3)]
        pairs = jnp.stack(
            [v.reshape(seq, share, 2 * width) for v in (keep, taken)], axis=1
        ).reshape(seq, cores * share, 2 * width)
        got = [pairs[0]] + [lax.ppermute(pairs[d], "seq", xor(seq, d)) for d in (1, 2, 3)]
    else:
        position, wanted = spread(lambda b: b, tokens, share, slot)
        asked = lax.all_to_all(wanted, ("seq", "sub"), split_axis=0, concat_axis=0, tiled=True)
        both = plain_projection(hidden_states, own)
        chip = core_split(local_moments(both, heads, dim).reshape(cores, mine, dim, dim), c)
        parts = [lax.psum(chip, "seq")]
        got = [
            lax.all_to_all(
                selected(asked, both), ("seq", "sub"), split_axis=0, concat_axis=0, tiled=True
            )
        ]

    solved = solve(parts, basis_here, tokens * peers)
    other = lax.ppermute(solved, "sub", SWAP)
    return finish(position, got, solved, other)


def solution(mesh):
    return jax.shard_map(
        per_device,
        mesh=mesh,
        in_specs=(
            P(("groups", "seq", "sub"), "head"),
            P(("seq", "sub"), "head"),
            P(("seq", "sub"), "head"),
            P("head", None, None),
            P(("groups", "seq", "sub")),
        ),
        out_specs=(P(("groups", "seq", "sub"), "head"), P(("groups", "seq", "sub"), "head")),
        check_vma=False,
    )
```

```python
import functools

import jax
import jax.numpy as jnp
from jax import lax
from jax.experimental import pallas as pl
from jax.experimental.pallas import tpu as pltpu
from jax.sharding import PartitionSpec as P

ridge_share = 0.05
SWAP = [(0, 1), (1, 0)]


def rotation(count, shift):
    return [(i, (i + shift) % count) for i in range(count)]


def xor(count, distance):
    return [(i, i ^ distance) for i in range(count)]


def pack(moments):
    first, second = moments[..., 0, :, :], moments[..., 1, :, :]
    dim = first.shape[-1]
    row = lax.broadcasted_iota(jnp.int32, (dim, dim), 0)
    col = lax.broadcasted_iota(jnp.int32, (dim, dim), 1)
    both = jnp.where(row >= col, first, second)
    diagonal = jnp.sum(jnp.where(row == col, second, 0.0), axis=-2, keepdims=True)
    return jnp.concatenate([both, jnp.broadcast_to(diagonal, (*both.shape[:-2], 8, dim))], axis=-2)


def unpack(packed):
    dim = packed.shape[1]
    row = lax.broadcasted_iota(jnp.int32, (dim, dim), 0)
    col = lax.broadcasted_iota(jnp.int32, (dim, dim), 1)
    both, diagonal = packed[:dim], packed[dim : dim + 1]
    turned = both.T
    first = jnp.where(row >= col, both, turned)
    second = jnp.where(row < col, both, jnp.where(row == col, diagonal, turned))
    return jnp.stack([first, second])


def solve_kernel(scale, parts, packed, *refs):
    m_refs, basis_ref, out_ref = refs[:parts], refs[parts], refs[parts + 1]
    heads, dim, _ = basis_ref.shape
    total = m_refs[0][...]
    for ref in m_refs[1:]:
        total = total + ref[...]
    total = total * scale
    if packed:
        total = unpack(total)
    row = lax.broadcasted_iota(jnp.int32, (1, dim, dim), 1)
    col = lax.broadcasted_iota(jnp.int32, (1, dim, dim), 2)
    diag = row == col
    trace = jnp.sum(jnp.where(diag, total, 0.0), axis=(1, 2), keepdims=True)
    work = total + jnp.where(diag, ridge_share * trace / dim, 0.0)
    tiles = [work[:, r : r + 8, :] for r in range(0, dim, 8)]
    lane = lax.broadcasted_iota(jnp.int32, (1, 1, dim), 2)
    sub = lax.broadcasted_iota(jnp.int32, (1, 8, 1), 1)
    for j in range(dim):
        t0, j0 = j // 8, j % 8
        pivot_row = tiles[t0][:, j0 : j0 + 1, :]
        inv = 1.0 / pivot_row[:, :, j : j + 1]
        scaled = jnp.where(lane == j, inv, pivot_row * inv)
        at = lane == j
        for t in range(t0, dim // 8):
            if t == t0 and j0 == 7:
                continue
            f = tiles[t][:, :, j : j + 1]
            if t == t0:
                f = jnp.where(sub > j0, f, 0.0)
                base = jnp.where(at & (sub > j0), 0.0, tiles[t])
            else:
                base = jnp.where(at, 0.0, tiles[t])
            tiles[t] = base - f * scaled
    work = jnp.concatenate(tiles, axis=1)
    pivots = jnp.sum(jnp.where(diag, work, 0.0), axis=2, keepdims=True)
    inverse = jnp.where(row > col, work, jnp.where(diag, 1.0, 0.0))
    scaled_basis = basis_ref[...] * lax.rsqrt(pivots)
    for h in range(heads):
        out_ref[h] = lax.dot_general(
            inverse[h].T,
            scaled_basis[h],
            (((1,), (0,)), ((), ())),
            precision=lax.Precision.HIGHEST,
            preferred_element_type=jnp.float32,
        )


def solve(parts, basis, token_total):
    heads, dim, rank = basis.shape
    vmem = pl.BlockSpec(memory_space=pltpu.VMEM)
    return pl.pallas_call(
        functools.partial(solve_kernel, 1.0 / token_total, len(parts), parts[0].ndim == 2),
        out_shape=jax.ShapeDtypeStruct((heads, dim, rank), jnp.float32),
        in_specs=[vmem] * (len(parts) + 1),
        out_specs=vmem,
        cost_estimate=pl.CostEstimate(flops=6000 * heads * dim**3 // 2, bytes_accessed=4 * heads * dim * dim, transcendentals=0),
    )(*parts, basis)


ALL_PIECES = [(d, k) for d in (1, 2, 3) for k in range(4)]
EARLY_PIECES = [(1, 0), (1, 1), (1, 2), (1, 3), (2, 0), (2, 1), (2, 2), (2, 3), (3, 0), (3, 2)]


def project_kernel(near, widths, last, *refs):
    refs = list(refs)
    x_own, xs = refs.pop(0), [refs.pop(0) for _ in widths]
    own, sib = refs.pop(0), refs.pop(0)
    pieces = {name: refs.pop(0) for name in (ALL_PIECES if last else EARLY_PIECES)}
    if last:
        acc_in, out_ref, xbuf, wbuf, xsem, wsem, acc = refs
    else:
        acc, xbuf, wbuf, xsem, wsem = refs
    g, s, h, c = (lax.axis_index(a) for a in ("groups", "seq", "head", "sub"))
    block = own.shape[0]
    half = block // 2
    count = 2 * near
    far_early = sum(widths) - (widths[-1] if last else 0)

    def x_copy(src, n):
        lanes = pl.ds(pl.multiple_of(n * half, half), half)
        return pltpu.make_async_copy(src, xbuf.at[:, lanes], xsem.at[n])

    def w_copy(src, n):
        return pltpu.make_async_copy(src, wbuf.at[pl.ds(pl.multiple_of(n * half, half), half)], wsem.at[n])

    def needed(n):
        dist = (n // 4) ^ s
        kind = jnp.where((n // 2) % 2 == c, 0, 2) + jnp.where(n % 2 == g, 0, 1)
        have = dist == 0
        for d, k in EARLY_PIECES:
            have = have | ((dist == d) & (kind == k))
        fresh = (n // near == h) | (n - (1 - h) * near < far_early)
        return (have & fresh) != last

    for i in range(near):

        @pl.when(needed(h * near + i))
        def _():
            x_copy(x_own.at[:, i * half : (i + 1) * half], h * near + i).start()

    for part in range(2):
        for core, src in ((c, own), (1 - c, sib)):
            n = s * 4 + core * 2 + part

            @pl.when(needed(n))
            def _():
                w_copy(src.at[pl.ds(part * half, half)], n).start()

    for (d, k), src in pieces.items():
        core = c if k < 2 else 1 - c
        n = (s ^ d) * 4 + core * 2 + (g if k % 2 == 0 else 1 - g)

        @pl.when(needed(n))
        def _():
            w_copy(src, n).start()

    n = (1 - h) * near
    for x_far, width in zip(xs, widths):
        for i in range(width):

            @pl.when(needed(n))
            def _():
                x_copy(x_far.at[:, i * half : (i + 1) * half], n).start()

            n = n + 1
    acc[...] = acc_in[...] if last else jnp.zeros_like(acc)

    @pl.loop(0, near + sum(widths))
    def _(i):
        n = lax.rem(i + h * near, count)

        @pl.when(needed(n))
        def _():
            x_copy(x_own.at[:, :half], n).wait()
            w_copy(own.at[pl.ds(0, half)], n).wait()
            off = pl.multiple_of(n * half, half)
            acc[...] += jnp.dot(
                xbuf[:, pl.ds(off, half)],
                wbuf[pl.ds(off, half), :],
                preferred_element_type=jnp.float32,
            )

    if last:
        out_ref[...] = acc[...].astype(out_ref.dtype)


def project(x, xs, own, sib, pieces, acc=None):
    last = acc is not None
    tokens, feats = x.shape
    block, width = own.shape
    near = 2 * feats // block
    widths = [2 * v.shape[1] // block for v in xs]
    given = [pieces[name] for name in (ALL_PIECES if last else EARLY_PIECES)]
    hbm, vmem = pl.BlockSpec(memory_space=pltpu.HBM), pl.BlockSpec(memory_space=pltpu.VMEM)
    free = 1 if last else 0
    args = [x, *xs, own, sib, *given]
    pinned = len(args) - free
    args = [pltpu.with_memory_space_constraint(v, pltpu.HBM) for v in args[:pinned]] + args[pinned:]
    specs = [hbm] * len(args)
    scratch = [
        pltpu.VMEM((tokens, 2 * feats), x.dtype),
        pltpu.VMEM((2 * feats, width), x.dtype),
        pltpu.SemaphoreType.DMA((2 * near,)),
        pltpu.SemaphoreType.DMA((2 * near,)),
    ]
    if last:
        args.append(acc)
        specs.append(vmem)
        scratch.append(pltpu.VMEM((tokens, width), jnp.float32))
    return pl.pallas_call(
        functools.partial(project_kernel, near, widths, last),
        out_shape=jax.ShapeDtypeStruct((tokens, width), jnp.bfloat16 if last else jnp.float32),
        in_specs=specs,
        out_specs=vmem,
        scratch_shapes=scratch,
        compiler_params=pltpu.CompilerParams(vmem_limit_bytes=36 << 20),
        cost_estimate=pl.CostEstimate(
            flops=2 * tokens * feats * width, bytes_accessed=16 << 20, transcendentals=0
        ),
    )(*args)


def gathered_projection(x, own, wanted):
    g, s = lax.axis_index("groups"), lax.axis_index("seq")
    inner = (s == 1) | (s == 2)
    block, feats = own.shape[0], x.shape[1]
    tie = lax.optimization_barrier

    def sub(value):
        return lax.ppermute(value, "sub", SWAP)

    def across(value):
        return lax.ppermute(value, "groups", SWAP)

    def along(value, *pairs):
        return lax.ppermute(value, "seq", pairs)

    def far(value):
        return lax.ppermute(value, "head", SWAP)

    unit = lax.dynamic_slice_in_dim(own, g * (block // 2), block // 2, axis=0)
    bounds = [0, 2, 4, 6, 8]

    def part(value, i):
        return value[:, bounds[i] * feats // 8 : bounds[i + 1] * feats // 8]

    x0 = far(part(x, 0))
    one = along(unit, (0, 1), (1, 0), (2, 3), (3, 2))
    mid = along(unit, (1, 2), (2, 1))
    x1 = far(part(tie(x), 1))
    one, mid, x_a, sib = tie((one, mid, x, sub(own)))
    third = part(x_a, 2)
    mid_two = along(one, (1, 2), (2, 1))
    out_two = along(mid, (1, 0), (2, 3))
    one_twin = across(one)
    mid_two, out_two, x0, x1, one_twin, third, one_b, x_b = tie(
        (mid_two, out_two, x0, x1, one_twin, third, one, x)
    )
    two = jnp.where(inner, mid_two, out_two)
    two, mid_two = tie((two, mid_two))
    out_three = along(mid_two, (1, 0), (2, 3))
    x2 = far(third)
    two_twin = across(two)
    fourth = part(x_b, 3)
    one_sib, one_twin_sib = sub(one_b), sub(one_twin)
    out_three, x2, two_twin, fourth, two_c = tie((out_three, x2, two_twin, fourth, two))
    three = jnp.where(inner, mid, out_three)
    twin = across(three)
    x3 = far(fourth)
    moved = {(1, 0): one, (1, 1): one_twin, (1, 2): one_sib, (1, 3): one_twin_sib}
    moved.update({(2, 0): two, (2, 1): two_twin, (3, 0): three})
    moved.update({(2, 2): sub(two_c), (2, 3): sub(two_twin), (3, 2): sub(three)})
    acc = project(x, [x0, x1, x2], own, sib, moved)
    acc, wanted = tie((acc, wanted))
    lists = jnp.stack([wanted] + [lax.ppermute(wanted, "seq", xor(4, d)) for d in (1, 2, 3)])
    twin_lists = sub(lists)
    twin, x3, acc = tie((twin, x3, acc))
    moved.update({(3, 1): twin, (3, 3): sub(twin)})
    return project(x, [x0, x1, x2, x3], own, sib, moved, acc), lists, twin_lists


def plain_projection(x, own):
    head = lax.axis_size("head")
    feats = x.shape[1]
    weights = lax.all_gather(own, ("seq", "sub"), axis=0, tiled=True)
    sums = None
    for d in range(head):
        rows = x if d == 0 else lax.ppermute(x, "head", rotation(head, -d))
        at = lax.rem(lax.axis_index("head") + d, head) * feats
        term = jnp.dot(
            rows,
            lax.dynamic_slice_in_dim(weights, at, feats, axis=0),
            preferred_element_type=jnp.float32,
        )
        sums = term if sums is None else sums + term
    return sums.astype(jnp.bfloat16)


def finish_kernel(position_ref, mine_ref, other_ref, *refs):
    got, coeff_ref, value_ref = refs[:-2], refs[-2], refs[-1]
    rows = jnp.concatenate([r[...] for r in got])
    tokens, width = rows.shape
    half = width // 2
    heads, dim, rank = mine_ref.shape
    place = lax.broadcasted_iota(jnp.int32, (tokens, tokens), 1)
    unpick = (position_ref[...] == place).astype(jnp.bfloat16)
    rows = jnp.dot(unpick, rows, preferred_element_type=jnp.float32)
    value_ref[...] = rows[:, half:].astype(value_ref.dtype)
    first = lax.axis_index("sub") == 0
    maps = [jnp.where(first, mine_ref[i], other_ref[i]) for i in range(heads)]
    maps += [jnp.where(first, other_ref[i], mine_ref[i]) for i in range(heads)]
    coeffs = [
        jnp.dot(
            rows[:, i * dim : (i + 1) * dim],
            m,
            precision=lax.Precision.HIGHEST,
            preferred_element_type=jnp.float32,
        )
        for i, m in enumerate(maps)
    ]
    coeff_ref[...] = jnp.concatenate(coeffs, axis=1).astype(coeff_ref.dtype)


def finish(position, got, solved, other):
    heads, dim, rank = solved.shape
    tokens = position.shape[0]
    vmem = pl.BlockSpec(memory_space=pltpu.VMEM)
    return pl.pallas_call(
        finish_kernel,
        out_shape=(
            jax.ShapeDtypeStruct((tokens, 2 * heads * rank), jnp.bfloat16),
            jax.ShapeDtypeStruct((tokens, 2 * heads * dim), jnp.bfloat16),
        ),
        in_specs=[vmem] * (3 + len(got)),
        out_specs=(vmem, vmem),
        compiler_params=pltpu.CompilerParams(vmem_limit_bytes=24 << 20),
    )(position[:, None], solved, other, *got)


def spread(order, tokens, share, slot):
    place = lax.iota(jnp.int32, tokens)
    block = slot // tokens
    before = (block[None, :] == block[:, None]) & (place[None, :] < place[:, None])
    position = order(block) * share + jnp.sum(before.astype(jnp.int32), axis=1)
    hits = position[:, None] == place[None, :]
    wanted = jnp.sum(jnp.where(hits, (slot - block * tokens)[:, None], 0), axis=0)
    return position, wanted


def selected(asked, rows):
    pick = (asked[:, None] == lax.iota(jnp.int32, rows.shape[0])[None, :]).astype(jnp.bfloat16)
    return jnp.dot(pick, rows, preferred_element_type=jnp.float32).astype(jnp.bfloat16)


def local_moments(both, heads, dim):
    keys = both[:, : heads * dim].reshape(both.shape[0], heads, dim)
    return jnp.einsum("thi,thj->hij", keys, keys, preferred_element_type=jnp.float32)


def core_split(values, c):
    keep = lax.dynamic_index_in_dim(values, c, 0, keepdims=False)
    give = lax.dynamic_index_in_dim(values, 1 - c, 0, keepdims=False)
    return keep + lax.ppermute(give, "sub", SWAP)


def per_device(hidden_states, key_w, value_w, basis, slot):
    tokens = hidden_states.shape[0]
    seq, head, cores = lax.axis_size("seq"), lax.axis_size("head"), lax.axis_size("sub")
    s, c = lax.axis_index("seq"), lax.axis_index("sub")
    peers = seq * cores
    share = tokens // peers
    heads, dim, rank = basis.shape
    mine = heads // cores
    width = heads * dim
    own = jnp.concatenate([key_w, value_w], axis=1)
    basis_here = lax.dynamic_slice_in_dim(basis, c * mine, mine, axis=0)

    if seq == 4 and head == 2 and lax.axis_size("groups") == 2 and mine == 2:
        position, wanted = spread(lambda b: b ^ (s * cores + c), tokens, share, slot)
        both, lists, twin_lists = gathered_projection(hidden_states, own, wanted)
        packed = pack(local_moments(both, heads, dim).reshape(cores, mine, dim, dim))
        chip = core_split(packed, c)
        near = [lists[d, 2 * d * share : (2 * d + 1) * share] for d in range(seq)]
        twin = [twin_lists[d, (2 * d + 1) * share : (2 * d + 2) * share] for d in range(seq)]
        give = selected(jnp.concatenate(twin), both)
        keep = selected(jnp.concatenate(near), both)
        taken = lax.ppermute(give, "sub", SWAP)
        parts = [chip] + [lax.ppermute(chip, "seq", xor(seq, d)) for d in (1, 2, 3)]
        pairs = jnp.stack(
            [v.reshape(seq, share, 2 * width) for v in (keep, taken)], axis=1
        ).reshape(seq, cores * share, 2 * width)
        got = [pairs[0]] + [lax.ppermute(pairs[d], "seq", xor(seq, d)) for d in (1, 2, 3)]
    else:
        position, wanted = spread(lambda b: b, tokens, share, slot)
        asked = lax.all_to_all(wanted, ("seq", "sub"), split_axis=0, concat_axis=0, tiled=True)
        both = plain_projection(hidden_states, own)
        chip = core_split(local_moments(both, heads, dim).reshape(cores, mine, dim, dim), c)
        parts = [lax.psum(chip, "seq")]
        got = [
            lax.all_to_all(
                selected(asked, both), ("seq", "sub"), split_axis=0, concat_axis=0, tiled=True
            )
        ]

    solved = solve(parts, basis_here, tokens * peers)
    other = lax.ppermute(solved, "sub", SWAP)
    return finish(position, got, solved, other)


def solution(mesh):
    return jax.shard_map(
        per_device,
        mesh=mesh,
        in_specs=(
            P(("groups", "seq", "sub"), "head"),
            P(("seq", "sub"), "head"),
            P(("seq", "sub"), "head"),
            P("head", None, None),
            P(("groups", "seq", "sub")),
        ),
        out_specs=(P(("groups", "seq", "sub"), "head"), P(("groups", "seq", "sub"), "head")),
        check_vma=False,
    )
```

```python
import functools

import jax
import jax.numpy as jnp
from jax import lax
from jax.experimental import pallas as pl
from jax.experimental.pallas import tpu as pltpu
from jax.sharding import PartitionSpec as P

ridge_share = 0.05
SWAP = [(0, 1), (1, 0)]


def rotation(count, shift):
    return [(i, (i + shift) % count) for i in range(count)]


def xor(count, distance):
    return [(i, i ^ distance) for i in range(count)]


def pack(moments):
    first, second = moments[..., 0, :, :], moments[..., 1, :, :]
    dim = first.shape[-1]
    row = lax.broadcasted_iota(jnp.int32, (dim, dim), 0)
    col = lax.broadcasted_iota(jnp.int32, (dim, dim), 1)
    both = jnp.where(row >= col, first, second)
    diagonal = jnp.sum(jnp.where(row == col, second, 0.0), axis=-2, keepdims=True)
    return jnp.concatenate([both, jnp.broadcast_to(diagonal, (*both.shape[:-2], 8, dim))], axis=-2)


def unpack(packed):
    dim = packed.shape[1]
    row = lax.broadcasted_iota(jnp.int32, (dim, dim), 0)
    col = lax.broadcasted_iota(jnp.int32, (dim, dim), 1)
    both, diagonal = packed[:dim], packed[dim : dim + 1]
    turned = both.T
    first = jnp.where(row >= col, both, turned)
    second = jnp.where(row < col, both, jnp.where(row == col, diagonal, turned))
    return jnp.stack([first, second])


def solve_kernel(scale, parts, packed, *refs):
    m_refs, basis_ref, out_ref = refs[:parts], refs[parts], refs[parts + 1]
    heads, dim, _ = basis_ref.shape
    total = m_refs[0][...]
    for ref in m_refs[1:]:
        total = total + ref[...]
    total = total * scale
    if packed:
        total = unpack(total)
    row = lax.broadcasted_iota(jnp.int32, (1, dim, dim), 1)
    col = lax.broadcasted_iota(jnp.int32, (1, dim, dim), 2)
    diag = row == col
    trace = jnp.sum(jnp.where(diag, total, 0.0), axis=(1, 2), keepdims=True)
    work = total + jnp.where(diag, ridge_share * trace / dim, 0.0)
    tiles = [work[:, r : r + 8, :] for r in range(0, dim, 8)]
    lane = lax.broadcasted_iota(jnp.int32, (1, 1, dim), 2)
    sub = lax.broadcasted_iota(jnp.int32, (1, 8, 1), 1)
    for j in range(dim):
        t0, j0 = j // 8, j % 8
        pivot_row = tiles[t0][:, j0 : j0 + 1, :]
        inv = 1.0 / pivot_row[:, :, j : j + 1]
        scaled = jnp.where(lane == j, inv, pivot_row * inv)
        at = lane == j
        for t in range(t0, dim // 8):
            if t == t0 and j0 == 7:
                continue
            f = tiles[t][:, :, j : j + 1]
            if t == t0:
                f = jnp.where(sub > j0, f, 0.0)
                base = jnp.where(at & (sub > j0), 0.0, tiles[t])
            else:
                base = jnp.where(at, 0.0, tiles[t])
            tiles[t] = base - f * scaled
    work = jnp.concatenate(tiles, axis=1)
    pivots = jnp.sum(jnp.where(diag, work, 0.0), axis=2, keepdims=True)
    inverse = jnp.where(row > col, work, jnp.where(diag, 1.0, 0.0))
    scaled_basis = basis_ref[...] * lax.rsqrt(pivots)
    for h in range(heads):
        out_ref[h] = lax.dot_general(
            inverse[h].T,
            scaled_basis[h],
            (((1,), (0,)), ((), ())),
            precision=lax.Precision.HIGHEST,
            preferred_element_type=jnp.float32,
        )


def solve(parts, basis, token_total):
    heads, dim, rank = basis.shape
    vmem = pl.BlockSpec(memory_space=pltpu.VMEM)
    return pl.pallas_call(
        functools.partial(solve_kernel, 1.0 / token_total, len(parts), parts[0].ndim == 2),
        out_shape=jax.ShapeDtypeStruct((heads, dim, rank), jnp.float32),
        in_specs=[vmem] * (len(parts) + 1),
        out_specs=vmem,
        cost_estimate=pl.CostEstimate(flops=6000 * heads * dim**3 // 2, bytes_accessed=4 * heads * dim * dim, transcendentals=0),
    )(*parts, basis)


ALL_PIECES = [(d, k) for d in (1, 2, 3) for k in range(4)]
EARLY_PIECES = [(1, 0), (1, 1), (1, 2), (1, 3), (2, 0), (2, 1), (2, 2), (2, 3), (3, 0), (3, 2)]


def project_kernel(near, widths, last, *refs):
    refs = list(refs)
    x_own, xs = refs.pop(0), [refs.pop(0) for _ in widths]
    own, sib = refs.pop(0), refs.pop(0)
    pieces = {name: refs.pop(0) for name in (ALL_PIECES if last else EARLY_PIECES)}
    if last:
        acc_in, out_ref, xbuf, wbuf, xsem, wsem, acc = refs
    else:
        acc, xbuf, wbuf, xsem, wsem = refs
    g, s, h, c = (lax.axis_index(a) for a in ("groups", "seq", "head", "sub"))
    block = own.shape[0]
    half = block // 2
    count = 2 * near
    far_early = sum(widths) - (widths[-1] if last else 0)

    def x_copy(src, n):
        lanes = pl.ds(pl.multiple_of(n * half, half), half)
        return pltpu.make_async_copy(src, xbuf.at[:, lanes], xsem.at[n])

    def w_copy(src, n):
        return pltpu.make_async_copy(src, wbuf.at[pl.ds(pl.multiple_of(n * half, half), half)], wsem.at[n])

    def needed(n):
        dist = (n // 4) ^ s
        kind = jnp.where((n // 2) % 2 == c, 0, 2) + jnp.where(n % 2 == g, 0, 1)
        have = dist == 0
        for d, k in EARLY_PIECES:
            have = have | ((dist == d) & (kind == k))
        fresh = (n // near == h) | (n - (1 - h) * near < far_early)
        return (have & fresh) != last

    for i in range(near):

        @pl.when(needed(h * near + i))
        def _():
            x_copy(x_own.at[:, i * half : (i + 1) * half], h * near + i).start()

    for part in range(2):
        for core, src in ((c, own), (1 - c, sib)):
            n = s * 4 + core * 2 + part

            @pl.when(needed(n))
            def _():
                w_copy(src.at[pl.ds(part * half, half)], n).start()

    for (d, k), src in pieces.items():
        core = c if k < 2 else 1 - c
        n = (s ^ d) * 4 + core * 2 + (g if k % 2 == 0 else 1 - g)

        @pl.when(needed(n))
        def _():
            w_copy(src, n).start()

    n = (1 - h) * near
    for x_far, width in zip(xs, widths):
        for i in range(width):

            @pl.when(needed(n))
            def _():
                x_copy(x_far.at[:, i * half : (i + 1) * half], n).start()

            n = n + 1
    acc[...] = acc_in[...] if last else jnp.zeros_like(acc)

    @pl.loop(0, near + sum(widths))
    def _(i):
        n = lax.rem(i + h * near, count)

        @pl.when(needed(n))
        def _():
            x_copy(x_own.at[:, :half], n).wait()
            w_copy(own.at[pl.ds(0, half)], n).wait()
            off = pl.multiple_of(n * half, half)
            acc[...] += jnp.dot(
                xbuf[:, pl.ds(off, half)],
                wbuf[pl.ds(off, half), :],
                preferred_element_type=jnp.float32,
            )

    if last:
        out_ref[...] = acc[...].astype(out_ref.dtype)


def project(x, xs, own, sib, pieces, acc=None):
    last = acc is not None
    tokens, feats = x.shape
    block, width = own.shape
    near = 2 * feats // block
    widths = [2 * v.shape[1] // block for v in xs]
    given = [pieces[name] for name in (ALL_PIECES if last else EARLY_PIECES)]
    hbm, vmem = pl.BlockSpec(memory_space=pltpu.HBM), pl.BlockSpec(memory_space=pltpu.VMEM)
    args = [x, *xs, own, sib, *given]
    free = (len(xs), len(args) - 1) if last else (len(xs),)
    args = [
        v if i in free else pltpu.with_memory_space_constraint(v, pltpu.HBM)
        for i, v in enumerate(args)
    ]
    specs = [hbm] * len(args)
    scratch = [
        pltpu.VMEM((tokens, 2 * feats), x.dtype),
        pltpu.VMEM((2 * feats, width), x.dtype),
        pltpu.SemaphoreType.DMA((2 * near,)),
        pltpu.SemaphoreType.DMA((2 * near,)),
    ]
    if last:
        args.append(acc)
        specs.append(vmem)
        scratch.append(pltpu.VMEM((tokens, width), jnp.float32))
    return pl.pallas_call(
        functools.partial(project_kernel, near, widths, last),
        out_shape=jax.ShapeDtypeStruct((tokens, width), jnp.bfloat16 if last else jnp.float32),
        in_specs=specs,
        out_specs=vmem,
        scratch_shapes=scratch,
        compiler_params=pltpu.CompilerParams(vmem_limit_bytes=36 << 20),
        cost_estimate=pl.CostEstimate(
            flops=2 * tokens * feats * width, bytes_accessed=16 << 20, transcendentals=0
        ),
    )(*args)


def gathered_projection(x, own, wanted):
    g, s = lax.axis_index("groups"), lax.axis_index("seq")
    inner = (s == 1) | (s == 2)
    block, feats = own.shape[0], x.shape[1]
    tie = lax.optimization_barrier

    def sub(value):
        return lax.ppermute(value, "sub", SWAP)

    def across(value):
        return lax.ppermute(value, "groups", SWAP)

    def along(value, *pairs):
        return lax.ppermute(value, "seq", pairs)

    def far(value):
        return lax.ppermute(value, "head", SWAP)

    unit = lax.dynamic_slice_in_dim(own, g * (block // 2), block // 2, axis=0)
    bounds = [0, 2, 4, 6, 8]

    def part(value, i):
        return value[:, bounds[i] * feats // 8 : bounds[i + 1] * feats // 8]

    x0 = far(part(x, 0))
    one = along(unit, (0, 1), (1, 0), (2, 3), (3, 2))
    mid = along(unit, (1, 2), (2, 1))
    x1 = far(part(tie(x), 1))
    one, mid, x_a, sib = tie((one, mid, x, sub(own)))
    third = part(x_a, 2)
    mid_two = along(one, (1, 2), (2, 1))
    out_two = along(mid, (1, 0), (2, 3))
    one_twin = across(one)
    mid_two, out_two, x0, x1, one_twin, third, one_b, x_b = tie(
        (mid_two, out_two, x0, x1, one_twin, third, one, x)
    )
    two = jnp.where(inner, mid_two, out_two)
    two, mid_two = tie((two, mid_two))
    out_three = along(mid_two, (1, 0), (2, 3))
    x2 = far(third)
    two_twin = across(two)
    fourth = part(x_b, 3)
    one_sib, one_twin_sib = sub(one_b), sub(one_twin)
    out_three, fourth, two_c = tie((out_three, fourth, two))
    three = jnp.where(inner, mid, out_three)
    twin = across(three)
    x3 = far(fourth)
    moved = {(1, 0): one, (1, 1): one_twin, (1, 2): one_sib, (1, 3): one_twin_sib}
    moved.update({(2, 0): two, (2, 1): two_twin, (3, 0): three})
    moved.update({(2, 2): sub(two_c), (2, 3): sub(two_twin), (3, 2): sub(three)})
    acc = project(x, [x0, x1, x2], own, sib, moved)
    acc, wanted = tie((acc, wanted))
    lists = jnp.stack([wanted] + [lax.ppermute(wanted, "seq", xor(4, d)) for d in (1, 2, 3)])
    twin_lists = sub(lists)
    twin, acc = tie((twin, acc))
    moved.update({(3, 1): twin, (3, 3): sub(twin)})
    return project(x, [x0, x1, x2, x3], own, sib, moved, acc), lists, twin_lists


def plain_projection(x, own):
    head = lax.axis_size("head")
    feats = x.shape[1]
    weights = lax.all_gather(own, ("seq", "sub"), axis=0, tiled=True)
    sums = None
    for d in range(head):
        rows = x if d == 0 else lax.ppermute(x, "head", rotation(head, -d))
        at = lax.rem(lax.axis_index("head") + d, head) * feats
        term = jnp.dot(
            rows,
            lax.dynamic_slice_in_dim(weights, at, feats, axis=0),
            preferred_element_type=jnp.float32,
        )
        sums = term if sums is None else sums + term
    return sums.astype(jnp.bfloat16)


def finish_kernel(position_ref, mine_ref, other_ref, *refs):
    got, coeff_ref, value_ref = refs[:-2], refs[-2], refs[-1]
    rows = jnp.concatenate([r[...] for r in got])
    tokens, width = rows.shape
    half = width // 2
    heads, dim, rank = mine_ref.shape
    place = lax.broadcasted_iota(jnp.int32, (tokens, tokens), 1)
    unpick = (position_ref[...] == place).astype(jnp.bfloat16)
    rows = jnp.dot(unpick, rows, preferred_element_type=jnp.float32)
    value_ref[...] = rows[:, half:].astype(value_ref.dtype)
    first = lax.axis_index("sub") == 0
    maps = [jnp.where(first, mine_ref[i], other_ref[i]) for i in range(heads)]
    maps += [jnp.where(first, other_ref[i], mine_ref[i]) for i in range(heads)]
    coeffs = [
        jnp.dot(
            rows[:, i * dim : (i + 1) * dim],
            m,
            precision=lax.Precision.HIGHEST,
            preferred_element_type=jnp.float32,
        )
        for i, m in enumerate(maps)
    ]
    coeff_ref[...] = jnp.concatenate(coeffs, axis=1).astype(coeff_ref.dtype)


def finish(position, got, solved, other):
    heads, dim, rank = solved.shape
    tokens = position.shape[0]
    vmem = pl.BlockSpec(memory_space=pltpu.VMEM)
    return pl.pallas_call(
        finish_kernel,
        out_shape=(
            jax.ShapeDtypeStruct((tokens, 2 * heads * rank), jnp.bfloat16),
            jax.ShapeDtypeStruct((tokens, 2 * heads * dim), jnp.bfloat16),
        ),
        in_specs=[vmem] * (3 + len(got)),
        out_specs=(vmem, vmem),
        compiler_params=pltpu.CompilerParams(vmem_limit_bytes=24 << 20),
    )(position[:, None], solved, other, *got)


def spread(order, tokens, share, slot):
    place = lax.iota(jnp.int32, tokens)
    block = slot // tokens
    before = (block[None, :] == block[:, None]) & (place[None, :] < place[:, None])
    position = order(block) * share + jnp.sum(before.astype(jnp.int32), axis=1)
    hits = position[:, None] == place[None, :]
    wanted = jnp.sum(jnp.where(hits, (slot - block * tokens)[:, None], 0), axis=0)
    return position, wanted


def selected(asked, rows):
    pick = (asked[:, None] == lax.iota(jnp.int32, rows.shape[0])[None, :]).astype(jnp.bfloat16)
    return jnp.dot(pick, rows, preferred_element_type=jnp.float32).astype(jnp.bfloat16)


def local_moments(both, heads, dim):
    keys = both[:, : heads * dim].reshape(both.shape[0], heads, dim)
    return jnp.einsum("thi,thj->hij", keys, keys, preferred_element_type=jnp.float32)


def core_split(values, c):
    keep = lax.dynamic_index_in_dim(values, c, 0, keepdims=False)
    give = lax.dynamic_index_in_dim(values, 1 - c, 0, keepdims=False)
    return keep + lax.ppermute(give, "sub", SWAP)


def per_device(hidden_states, key_w, value_w, basis, slot):
    tokens = hidden_states.shape[0]
    seq, head, cores = lax.axis_size("seq"), lax.axis_size("head"), lax.axis_size("sub")
    s, c = lax.axis_index("seq"), lax.axis_index("sub")
    peers = seq * cores
    share = tokens // peers
    heads, dim, rank = basis.shape
    mine = heads // cores
    width = heads * dim
    own = jnp.concatenate([key_w, value_w], axis=1)
    basis_here = lax.dynamic_slice_in_dim(basis, c * mine, mine, axis=0)

    if seq == 4 and head == 2 and lax.axis_size("groups") == 2 and mine == 2:
        position, wanted = spread(lambda b: b ^ (s * cores + c), tokens, share, slot)
        both, lists, twin_lists = gathered_projection(hidden_states, own, wanted)
        packed = pack(local_moments(both, heads, dim).reshape(cores, mine, dim, dim))
        chip = core_split(packed, c)
        near = [lists[d, 2 * d * share : (2 * d + 1) * share] for d in range(seq)]
        twin = [twin_lists[d, (2 * d + 1) * share : (2 * d + 2) * share] for d in range(seq)]
        give = selected(jnp.concatenate(twin), both)
        keep = selected(jnp.concatenate(near), both)
        taken = lax.ppermute(give, "sub", SWAP)
        parts = [chip] + [lax.ppermute(chip, "seq", xor(seq, d)) for d in (1, 2, 3)]
        pairs = jnp.stack(
            [v.reshape(seq, share, 2 * width) for v in (keep, taken)], axis=1
        ).reshape(seq, cores * share, 2 * width)
        got = [pairs[0]] + [lax.ppermute(pairs[d], "seq", xor(seq, d)) for d in (1, 2, 3)]
    else:
        position, wanted = spread(lambda b: b, tokens, share, slot)
        asked = lax.all_to_all(wanted, ("seq", "sub"), split_axis=0, concat_axis=0, tiled=True)
        both = plain_projection(hidden_states, own)
        chip = core_split(local_moments(both, heads, dim).reshape(cores, mine, dim, dim), c)
        parts = [lax.psum(chip, "seq")]
        got = [
            lax.all_to_all(
                selected(asked, both), ("seq", "sub"), split_axis=0, concat_axis=0, tiled=True
            )
        ]

    solved = solve(parts, basis_here, tokens * peers)
    other = lax.ppermute(solved, "sub", SWAP)
    return finish(position, got, solved, other)


def solution(mesh):
    return jax.shard_map(
        per_device,
        mesh=mesh,
        in_specs=(
            P(("groups", "seq", "sub"), "head"),
            P(("seq", "sub"), "head"),
            P(("seq", "sub"), "head"),
            P("head", None, None),
            P(("groups", "seq", "sub")),
        ),
        out_specs=(P(("groups", "seq", "sub"), "head"), P(("groups", "seq", "sub"), "head")),
        check_vma=False,
    )
```

```python
import functools

import jax
import jax.numpy as jnp
from jax import lax
from jax.experimental import pallas as pl
from jax.experimental.pallas import tpu as pltpu
from jax.sharding import PartitionSpec as P

ridge_share = 0.05
SWAP = [(0, 1), (1, 0)]


def rotation(count, shift):
    return [(i, (i + shift) % count) for i in range(count)]


def xor(count, distance):
    return [(i, i ^ distance) for i in range(count)]


def pack(moments):
    first, second = moments[..., 0, :, :], moments[..., 1, :, :]
    dim = first.shape[-1]
    row = lax.broadcasted_iota(jnp.int32, (dim, dim), 0)
    col = lax.broadcasted_iota(jnp.int32, (dim, dim), 1)
    both = jnp.where(row >= col, first, second)
    diagonal = jnp.sum(jnp.where(row == col, second, 0.0), axis=-2, keepdims=True)
    return jnp.concatenate([both, jnp.broadcast_to(diagonal, (*both.shape[:-2], 8, dim))], axis=-2)


def unpack(packed):
    dim = packed.shape[1]
    row = lax.broadcasted_iota(jnp.int32, (dim, dim), 0)
    col = lax.broadcasted_iota(jnp.int32, (dim, dim), 1)
    both, diagonal = packed[:dim], packed[dim : dim + 1]
    turned = both.T
    first = jnp.where(row >= col, both, turned)
    second = jnp.where(row < col, both, jnp.where(row == col, diagonal, turned))
    return jnp.stack([first, second])


def solve_kernel(scale, parts, packed, *refs):
    m_refs, basis_ref, out_ref = refs[:parts], refs[parts], refs[parts + 1]
    heads, dim, _ = basis_ref.shape
    total = m_refs[0][...]
    for ref in m_refs[1:]:
        total = total + ref[...]
    total = total * scale
    if packed:
        total = unpack(total)
    row = lax.broadcasted_iota(jnp.int32, (1, dim, dim), 1)
    col = lax.broadcasted_iota(jnp.int32, (1, dim, dim), 2)
    diag = row == col
    trace = jnp.sum(jnp.where(diag, total, 0.0), axis=(1, 2), keepdims=True)
    work = total + jnp.where(diag, ridge_share * trace / dim, 0.0)
    tiles = [work[:, r : r + 8, :] for r in range(0, dim, 8)]
    lane = lax.broadcasted_iota(jnp.int32, (1, 1, dim), 2)
    sub = lax.broadcasted_iota(jnp.int32, (1, 8, 1), 1)
    for j in range(dim):
        t0, j0 = j // 8, j % 8
        pivot_row = tiles[t0][:, j0 : j0 + 1, :]
        inv = 1.0 / pivot_row[:, :, j : j + 1]
        scaled = jnp.where(lane == j, inv, pivot_row * inv)
        at = lane == j
        for t in range(t0, dim // 8):
            if t == t0 and j0 == 7:
                continue
            f = tiles[t][:, :, j : j + 1]
            if t == t0:
                f = jnp.where(sub > j0, f, 0.0)
                base = jnp.where(at & (sub > j0), 0.0, tiles[t])
            else:
                base = jnp.where(at, 0.0, tiles[t])
            tiles[t] = base - f * scaled
    work = jnp.concatenate(tiles, axis=1)
    pivots = jnp.sum(jnp.where(diag, work, 0.0), axis=2, keepdims=True)
    inverse = jnp.where(row > col, work, jnp.where(diag, 1.0, 0.0))
    scaled_basis = basis_ref[...] * lax.rsqrt(pivots)
    for h in range(heads):
        out_ref[h] = lax.dot_general(
            inverse[h].T,
            scaled_basis[h],
            (((1,), (0,)), ((), ())),
            precision=lax.Precision.HIGHEST,
            preferred_element_type=jnp.float32,
        )


def solve(parts, basis, token_total):
    heads, dim, rank = basis.shape
    vmem = pl.BlockSpec(memory_space=pltpu.VMEM)
    return pl.pallas_call(
        functools.partial(solve_kernel, 1.0 / token_total, len(parts), parts[0].ndim == 2),
        out_shape=jax.ShapeDtypeStruct((heads, dim, rank), jnp.float32),
        in_specs=[vmem] * (len(parts) + 1),
        out_specs=vmem,
        cost_estimate=pl.CostEstimate(flops=6000 * heads * dim**3 // 2, bytes_accessed=4 * heads * dim * dim, transcendentals=0),
    )(*parts, basis)


ALL_PIECES = [(d, k) for d in (1, 2, 3) for k in range(4)]
EARLY_PIECES = [(1, 0), (1, 1), (1, 2), (1, 3), (2, 0), (2, 1), (2, 2), (2, 3), (3, 0), (3, 2)]


def project_kernel(near, widths, last, *refs):
    refs = list(refs)
    x_own, xs = refs.pop(0), [refs.pop(0) for _ in widths]
    own, sib = refs.pop(0), refs.pop(0)
    pieces = {name: refs.pop(0) for name in (ALL_PIECES if last else EARLY_PIECES)}
    if last:
        acc_in, out_ref, xbuf, wbuf, xsem, wsem, acc = refs
    else:
        acc, xbuf, wbuf, xsem, wsem = refs
    g, s, h, c = (lax.axis_index(a) for a in ("groups", "seq", "head", "sub"))
    block = own.shape[0]
    half = block // 2
    count = 2 * near
    far_early = sum(widths) - (widths[-1] if last else 0)

    def x_copy(src, n):
        lanes = pl.ds(pl.multiple_of(n * half, half), half)
        return pltpu.make_async_copy(src, xbuf.at[:, lanes], xsem.at[n])

    def w_copy(src, n):
        return pltpu.make_async_copy(src, wbuf.at[pl.ds(pl.multiple_of(n * half, half), half)], wsem.at[n])

    def needed(n):
        dist = (n // 4) ^ s
        kind = jnp.where((n // 2) % 2 == c, 0, 2) + jnp.where(n % 2 == g, 0, 1)
        have = dist == 0
        for d, k in EARLY_PIECES:
            have = have | ((dist == d) & (kind == k))
        fresh = (n // near == h) | (n - (1 - h) * near < far_early)
        return (have & fresh) != last

    for i in range(near):

        @pl.when(needed(h * near + i))
        def _():
            x_copy(x_own.at[:, i * half : (i + 1) * half], h * near + i).start()

    for part in range(2):
        for core, src in ((c, own), (1 - c, sib)):
            n = s * 4 + core * 2 + part

            @pl.when(needed(n))
            def _():
                w_copy(src.at[pl.ds(part * half, half)], n).start()

    for (d, k), src in pieces.items():
        core = c if k < 2 else 1 - c
        n = (s ^ d) * 4 + core * 2 + (g if k % 2 == 0 else 1 - g)

        @pl.when(needed(n))
        def _():
            w_copy(src, n).start()

    n = (1 - h) * near
    for x_far, width in zip(xs, widths):
        for i in range(width):

            @pl.when(needed(n))
            def _():
                x_copy(x_far.at[:, i * half : (i + 1) * half], n).start()

            n = n + 1
    acc[...] = acc_in[...] if last else jnp.zeros_like(acc)

    @pl.loop(0, near + sum(widths))
    def _(i):
        n = lax.rem(i + h * near, count)

        @pl.when(needed(n))
        def _():
            x_copy(x_own.at[:, :half], n).wait()
            w_copy(own.at[pl.ds(0, half)], n).wait()
            off = pl.multiple_of(n * half, half)
            acc[...] += jnp.dot(
                xbuf[:, pl.ds(off, half)],
                wbuf[pl.ds(off, half), :],
                preferred_element_type=jnp.float32,
            )

    if last:
        out_ref[...] = acc[...].astype(out_ref.dtype)


def project(x, xs, own, sib, pieces, acc=None):
    last = acc is not None
    tokens, feats = x.shape
    block, width = own.shape
    near = 2 * feats // block
    widths = [2 * v.shape[1] // block for v in xs]
    given = [pieces[name] for name in (ALL_PIECES if last else EARLY_PIECES)]
    hbm, vmem = pl.BlockSpec(memory_space=pltpu.HBM), pl.BlockSpec(memory_space=pltpu.VMEM)
    args = [x, *xs, own, sib, *given]
    free = (len(xs), len(args) - 1) if last else (len(xs),)
    args = [
        v if i in free else pltpu.with_memory_space_constraint(v, pltpu.HBM)
        for i, v in enumerate(args)
    ]
    specs = [hbm] * len(args)
    scratch = [
        pltpu.VMEM((tokens, 2 * feats), x.dtype),
        pltpu.VMEM((2 * feats, width), x.dtype),
        pltpu.SemaphoreType.DMA((2 * near,)),
        pltpu.SemaphoreType.DMA((2 * near,)),
    ]
    if last:
        args.append(acc)
        specs.append(vmem)
        scratch.append(pltpu.VMEM((tokens, width), jnp.float32))
    return pl.pallas_call(
        functools.partial(project_kernel, near, widths, last),
        out_shape=jax.ShapeDtypeStruct((tokens, width), jnp.bfloat16 if last else jnp.float32),
        in_specs=specs,
        out_specs=vmem,
        scratch_shapes=scratch,
        compiler_params=pltpu.CompilerParams(vmem_limit_bytes=33 << 20),
        cost_estimate=pl.CostEstimate(
            flops=2 * tokens * feats * width, bytes_accessed=16 << 20, transcendentals=0
        ),
    )(*args)


def gathered_projection(x, own, wanted):
    g, s = lax.axis_index("groups"), lax.axis_index("seq")
    inner = (s == 1) | (s == 2)
    block, feats = own.shape[0], x.shape[1]
    tie = lax.optimization_barrier

    def sub(value):
        return lax.ppermute(value, "sub", SWAP)

    def across(value):
        return lax.ppermute(value, "groups", SWAP)

    def along(value, *pairs):
        return lax.ppermute(value, "seq", pairs)

    def far(value):
        return lax.ppermute(value, "head", SWAP)

    unit = lax.dynamic_slice_in_dim(own, g * (block // 2), block // 2, axis=0)
    bounds = [0, 2, 4, 6, 8]

    def part(value, i):
        return value[:, bounds[i] * feats // 8 : bounds[i + 1] * feats // 8]

    x0 = far(part(x, 0))
    one = along(unit, (0, 1), (1, 0), (2, 3), (3, 2))
    mid = along(unit, (1, 2), (2, 1))
    x1 = far(part(tie(x), 1))
    one, mid, x_a, sib = tie((one, mid, x, sub(own)))
    third = part(x_a, 2)
    mid_two = along(one, (1, 2), (2, 1))
    out_two = along(mid, (1, 0), (2, 3))
    one_twin = across(one)
    mid_two, out_two, x0, x1, one_twin, third, one_b, x_b = tie(
        (mid_two, out_two, x0, x1, one_twin, third, one, x)
    )
    two = jnp.where(inner, mid_two, out_two)
    two, mid_two = tie((two, mid_two))
    out_three = along(mid_two, (1, 0), (2, 3))
    x2 = far(third)
    two_twin = across(two)
    fourth = part(x_b, 3)
    one_sib, one_twin_sib = sub(one_b), sub(one_twin)
    out_three, fourth, two_c = tie((out_three, fourth, two))
    three = jnp.where(inner, mid, out_three)
    twin = across(three)
    x3 = far(fourth)
    moved = {(1, 0): one, (1, 1): one_twin, (1, 2): one_sib, (1, 3): one_twin_sib}
    moved.update({(2, 0): two, (2, 1): two_twin, (3, 0): three})
    moved.update({(2, 2): sub(two_c), (2, 3): sub(two_twin), (3, 2): sub(three)})
    acc = project(x, [x0, x1, x2], own, sib, moved)
    acc, wanted = tie((acc, wanted))
    lists = jnp.stack([wanted] + [lax.ppermute(wanted, "seq", xor(4, d)) for d in (1, 2, 3)])
    twin_lists = sub(lists)
    twin, acc = tie((twin, acc))
    moved.update({(3, 1): twin, (3, 3): sub(twin)})
    return project(x, [x0, x1, x2, x3], own, sib, moved, acc), lists, twin_lists


def plain_projection(x, own):
    head = lax.axis_size("head")
    feats = x.shape[1]
    weights = lax.all_gather(own, ("seq", "sub"), axis=0, tiled=True)
    sums = None
    for d in range(head):
        rows = x if d == 0 else lax.ppermute(x, "head", rotation(head, -d))
        at = lax.rem(lax.axis_index("head") + d, head) * feats
        term = jnp.dot(
            rows,
            lax.dynamic_slice_in_dim(weights, at, feats, axis=0),
            preferred_element_type=jnp.float32,
        )
        sums = term if sums is None else sums + term
    return sums.astype(jnp.bfloat16)


def finish_kernel(position_ref, mine_ref, other_ref, *refs):
    got, coeff_ref, value_ref = refs[:-2], refs[-2], refs[-1]
    rows = jnp.concatenate([r[...] for r in got])
    tokens, width = rows.shape
    half = width // 2
    heads, dim, rank = mine_ref.shape
    place = lax.broadcasted_iota(jnp.int32, (tokens, tokens), 1)
    unpick = (position_ref[...] == place).astype(jnp.bfloat16)
    rows = jnp.dot(unpick, rows, preferred_element_type=jnp.float32)
    value_ref[...] = rows[:, half:].astype(value_ref.dtype)
    first = lax.axis_index("sub") == 0
    maps = [jnp.where(first, mine_ref[i], other_ref[i]) for i in range(heads)]
    maps += [jnp.where(first, other_ref[i], mine_ref[i]) for i in range(heads)]
    coeffs = [
        jnp.dot(
            rows[:, i * dim : (i + 1) * dim],
            m,
            precision=lax.Precision.HIGHEST,
            preferred_element_type=jnp.float32,
        )
        for i, m in enumerate(maps)
    ]
    coeff_ref[...] = jnp.concatenate(coeffs, axis=1).astype(coeff_ref.dtype)


def finish(position, got, solved, other):
    heads, dim, rank = solved.shape
    tokens = position.shape[0]
    vmem = pl.BlockSpec(memory_space=pltpu.VMEM)
    return pl.pallas_call(
        finish_kernel,
        out_shape=(
            jax.ShapeDtypeStruct((tokens, 2 * heads * rank), jnp.bfloat16),
            jax.ShapeDtypeStruct((tokens, 2 * heads * dim), jnp.bfloat16),
        ),
        in_specs=[vmem] * (3 + len(got)),
        out_specs=(vmem, vmem),
        compiler_params=pltpu.CompilerParams(vmem_limit_bytes=24 << 20),
    )(position[:, None], solved, other, *got)


def spread(order, tokens, share, slot):
    place = lax.iota(jnp.int32, tokens)
    block = slot // tokens
    before = (block[None, :] == block[:, None]) & (place[None, :] < place[:, None])
    position = order(block) * share + jnp.sum(before.astype(jnp.int32), axis=1)
    hits = position[:, None] == place[None, :]
    wanted = jnp.sum(jnp.where(hits, (slot - block * tokens)[:, None], 0), axis=0)
    return position, wanted


def selected(asked, rows):
    pick = (asked[:, None] == lax.iota(jnp.int32, rows.shape[0])[None, :]).astype(jnp.bfloat16)
    return jnp.dot(pick, rows, preferred_element_type=jnp.float32).astype(jnp.bfloat16)


def local_moments(both, heads, dim):
    keys = both[:, : heads * dim].reshape(both.shape[0], heads, dim)
    return jnp.einsum("thi,thj->hij", keys, keys, preferred_element_type=jnp.float32)


def core_split(values, c):
    keep = lax.dynamic_index_in_dim(values, c, 0, keepdims=False)
    give = lax.dynamic_index_in_dim(values, 1 - c, 0, keepdims=False)
    return keep + lax.ppermute(give, "sub", SWAP)


def per_device(hidden_states, key_w, value_w, basis, slot):
    tokens = hidden_states.shape[0]
    seq, head, cores = lax.axis_size("seq"), lax.axis_size("head"), lax.axis_size("sub")
    s, c = lax.axis_index("seq"), lax.axis_index("sub")
    peers = seq * cores
    share = tokens // peers
    heads, dim, rank = basis.shape
    mine = heads // cores
    width = heads * dim
    own = jnp.concatenate([key_w, value_w], axis=1)
    basis_here = lax.dynamic_slice_in_dim(basis, c * mine, mine, axis=0)

    if seq == 4 and head == 2 and lax.axis_size("groups") == 2 and mine == 2:
        position, wanted = spread(lambda b: b ^ (s * cores + c), tokens, share, slot)
        both, lists, twin_lists = gathered_projection(hidden_states, own, wanted)
        packed = pack(local_moments(both, heads, dim).reshape(cores, mine, dim, dim))
        chip = core_split(packed, c)
        near = [lists[d, 2 * d * share : (2 * d + 1) * share] for d in range(seq)]
        twin = [twin_lists[d, (2 * d + 1) * share : (2 * d + 2) * share] for d in range(seq)]
        give = selected(jnp.concatenate(twin), both)
        keep = selected(jnp.concatenate(near), both)
        taken = lax.ppermute(give, "sub", SWAP)
        parts = [chip] + [lax.ppermute(chip, "seq", xor(seq, d)) for d in (1, 2, 3)]
        pairs = jnp.stack(
            [v.reshape(seq, share, 2 * width) for v in (keep, taken)], axis=1
        ).reshape(seq, cores * share, 2 * width)
        got = [pairs[0]] + [lax.ppermute(pairs[d], "seq", xor(seq, d)) for d in (1, 2, 3)]
    else:
        position, wanted = spread(lambda b: b, tokens, share, slot)
        asked = lax.all_to_all(wanted, ("seq", "sub"), split_axis=0, concat_axis=0, tiled=True)
        both = plain_projection(hidden_states, own)
        chip = core_split(local_moments(both, heads, dim).reshape(cores, mine, dim, dim), c)
        parts = [lax.psum(chip, "seq")]
        got = [
            lax.all_to_all(
                selected(asked, both), ("seq", "sub"), split_axis=0, concat_axis=0, tiled=True
            )
        ]

    solved = solve(parts, basis_here, tokens * peers)
    other = lax.ppermute(solved, "sub", SWAP)
    return finish(position, got, solved, other)


def solution(mesh):
    return jax.shard_map(
        per_device,
        mesh=mesh,
        in_specs=(
            P(("groups", "seq", "sub"), "head"),
            P(("seq", "sub"), "head"),
            P(("seq", "sub"), "head"),
            P("head", None, None),
            P(("groups", "seq", "sub")),
        ),
        out_specs=(P(("groups", "seq", "sub"), "head"), P(("groups", "seq", "sub"), "head")),
        check_vma=False,
    )
```
